32 devices in a mesh: fsdp: 16 (over z, y, core), tensor: 2 (over x).
Axes of the slice: x: 2, y: 2, z: 4, core: 2. Of those that a mesh axis runs over, the one named last changes fastest.
Arguments:
- tokens: bfloat16 [1152, 32768], P('tensor', 'fsdp'), may hold values from -6 to 6
- condition: bfloat16 [128, 1152], P('fsdp'), may hold values from -6 to 6
- grid_shapes: int32 [128, 2], P('fsdp'), may hold values from 4 to 64, as said below
- cotangent: bfloat16 [1152, 32768], P('tensor', 'fsdp'), may hold values from -6 to 6
- modulation_weight: bfloat16 [1152, 6, 1152], P('fsdp', None, 'tensor'), may hold values from -0.1875 to 0.1875
- modulation_bias: bfloat16 [6, 1152], P(None, 'tensor'), may hold values from -3 to 3
- attend_weight: bfloat16 [1152, 3, 1152], P('fsdp', None, 'tensor'), may hold values from -0.1875 to 0.1875
- attend_bias: bfloat16 [2, 1152], P(None, 'tensor'), may hold values from -3 to 3
- merge_weight: bfloat16 [1152, 1152], P('tensor', 'fsdp'), may hold values from -0.75 to 0.75
- merge_bias: bfloat16 [1152], P('tensor'), may hold values from -3 to 3
- expand_weight: bfloat16 [1152, 4608], P('fsdp', 'tensor'), may hold values from -0.1875 to 0.1875
- expand_bias: bfloat16 [4608], P('tensor'), may hold values from -3 to 3
- reduce_weight: bfloat16 [4608, 1152], P('tensor', 'fsdp'), may hold values from -0.09375 to 0.09375
- reduce_bias: bfloat16 [1152], P('tensor'), may hold values from -3 to 3
Outputs:
- output: float32 [1152, 32768], P('tensor', 'fsdp')
- tokens_grad: float32 [1152, 32768], P('tensor', 'fsdp')
- condition_grad: float32 [128, 1152], P('fsdp', 'tensor')
- modulation_weight_grad: float32 [1152, 6, 1152], P('fsdp', None, 'tensor')
- modulation_bias_grad: float32 [6, 1152], P(None, 'tensor')
- attend_weight_grad: float32 [1152, 3, 1152], P('fsdp', None, 'tensor')
- attend_bias_grad: float32 [2, 1152], P(None, 'tensor')
- merge_weight_grad: float32 [1152, 1152], P('tensor', 'fsdp')
- merge_bias_grad: float32 [1152], P('tensor')
- expand_weight_grad: float32 [1152, 4608], P('fsdp', 'tensor')
- expand_bias_grad: float32 [4608], P('tensor')
- reduce_weight_grad: float32 [4608, 1152], P('tensor', 'fsdp')
- reduce_bias_grad: float32 [1152], P('tensor')
The draws below stay inside these ranges and needn't reach their ends.
Inputs may be any that keep to these rules, and one draw needn't show every extreme that they name: `grid_shapes`: each row gives an image's patch rows, then patch columns; their product is at most 256, and the first rows times columns slots of the image hold its patches in row-major order.
All inputs are finite; a program needn't handle non-finite values.
Results may differ from the reference program's by a relative error of at most 0.018.
The reference program's roundings to bfloat16 on the way count: a program that leaves them out, or rounds other values in their place, can miss the bound.
Values may be sent and summed in bfloat16 or wider, within the bound.
No kernel may reach another device: no remote copies, remote signals or barrier semaphores. Data moves between devices by JAX's collectives and lax.ppermute only.
A program may use at most 320 MiB of HBM per device.

```python
import math
import jax
import jax.numpy as jnp
from jax import lax

D = 1152
H = 16
HD = 72
FF = 4608
SLOTS = 256
IMAGES = 128
TOKENS = 32768


def draw_grid_shapes(key, part):
    fewest = max(SLOTS // 16, 1)
    widest = SLOTS // 4
    columns = jax.random.randint(jax.random.fold_in(key, 11), (IMAGES,), fewest, widest + 1)
    columns = columns.at[0].set(fewest).at[1].set(widest)
    rows_count = SLOTS // columns
    return jnp.stack([rows_count, columns], axis=1).astype(jnp.int32)


def spiked(values, stream_key, source, target, shards_of, factor):
    def block_of(dim):
        return (jnp.arange(values.shape[dim]) // (values.shape[dim] // shards_of)).reshape((-1,) + (1,) * (values.ndim - 1 - dim))

    one_side = jax.random.permutation(stream_key, shards_of)[block_of(target)]
    second = (block_of(target) + shards_of // 2) % shards_of
    return jnp.where((block_of(source) == one_side) | (block_of(source) == second), factor * values, values)


def level_of(own_key, shape, cuts, low, top_value):
    def one(dim, blocks):
        draws = jax.random.uniform(jax.random.fold_in(jax.random.fold_in(own_key, 6), dim), (blocks,), jnp.float32, low / len(cuts), top_value / len(cuts))
        return jnp.repeat(jnp.exp(draws), shape[dim] // blocks).reshape((-1,) + (1,) * (len(shape) - dim - 1))

    loudness = one(*cuts[0])
    for cut in cuts[1:]:
        loudness = loudness * one(*cut)
    return loudness


def gaussian(key, shape, scale, bound, pieces=(), kind=jnp.bfloat16):
    loudness = level_of(key, shape, pieces, -0.22, 0.18) if pieces else 1.0
    array = jax.random.normal(key, shape, jnp.float32) * scale * loudness
    return jnp.minimum(jnp.maximum(array, -bound), bound).astype(kind)


def gaussian_with(rng, extent, width, bound, shards, heavy, kind=jnp.bfloat16):
    drawn = width * jax.random.normal(rng, extent, jnp.float32)
    if shards:
        drawn = drawn * level_of(rng, extent, shards, -0.22, 0.18)
    return jnp.clip(spiked(drawn, jax.random.fold_in(rng, 3), *heavy), -bound, bound).astype(kind)


def setup_inputs(seed: int = 0) -> dict:
    splits = jax.random.split(jax.random.key(seed), 15)
    return {
        "tokens": gaussian(splits[0], (D, TOKENS), 1.0, 6.0, ((0, 2), (1, 16))),
        "condition": gaussian(splits[1], (IMAGES, D), 1.0, 6.0, ((0, 16),)),
        "grid_shapes": draw_grid_shapes(jax.random.fold_in(splits[14], 71), 0),
        "cotangent": gaussian_with(splits[3], (D, TOKENS), 1.0, 6.0, ((0, 2), (1, 16)), (1, 0, 16, 2.0)),
        "modulation_weight": gaussian(splits[4], (D, 6, D), D ** -0.5, 0.1875, ((0, 16), (2, 2))),
        "modulation_bias": gaussian(splits[5], (6, D), 0.5, 3.0, ((1, 2),)),
        "attend_weight": gaussian(splits[6], (D, 3, H * HD), D ** -0.5, 0.1875, ((0, 16), (2, 2))),
        "attend_bias": gaussian(splits[7], (2, H * HD), 0.5, 3.0, ((1, 2),)),
        "merge_weight": gaussian(splits[8], (H * HD, D), (D // 16) ** -0.5, 0.75, ((0, 2), (1, 16))),
        "merge_bias": gaussian(splits[9], (D,), 0.5, 3.0, ((0, 2),)),
        "expand_weight": gaussian(splits[10], (D, FF), D ** -0.5, 0.1875, ((0, 16), (1, 2))),
        "expand_bias": gaussian(splits[11], (FF,), 0.5, 3.0, ((0, 2),)),
        "reduce_weight": gaussian(splits[12], (FF, D), FF ** -0.5, 0.09375, ((0, 2), (1, 16))),
        "reduce_bias": gaussian(splits[13], (D,), 0.5, 3.0, ((0, 2),)),
    }


EPSILON = 1e-06
NEGATIVE = -1e+30
HIGHEST = lax.Precision.HIGHEST

@jax.custom_vjp
def low(v):
    return lax.optimization_barrier(v.astype(jnp.bfloat16)).astype(jnp.float32)

@jax.custom_vjp
def low_back(v):
    return v

def low_keep(v):
    return (low(v), None)

def low_pass(kept, grad):
    return (grad,)

def back_keep(v):
    return (v, None)

def back_low(kept, grad):
    return (low(grad),)
low.defvjp(low_keep, low_pass)
low_back.defvjp(back_keep, back_low)

def position_table(grid_shapes, offset, columns):
    slot_line = jnp.arange(SLOTS, dtype=jnp.int32)
    across = grid_shapes[:, 1]
    row_index = slot_line[None, :] // across[:, None]
    col_index = slot_line[None, :] % across[:, None]
    channel = offset + jnp.arange(columns, dtype=jnp.int32)
    quarter = channel // (D // 4)
    within = channel % (D // 4)
    frequency = jnp.exp(within.astype(jnp.float32) * (-math.log(10000.0) / (D // 4)))
    row_angle = row_index.astype(jnp.float32)[:, :, None] * frequency
    col_angle = col_index.astype(jnp.float32)[:, :, None] * frequency
    return jnp.where(quarter == 0, jnp.sin(row_angle), jnp.where(quarter == 1, jnp.cos(row_angle), jnp.where(quarter == 2, jnp.sin(col_angle), jnp.cos(col_angle))))

def slot_present(grid_shapes):
    slot_line = jnp.arange(SLOTS, dtype=jnp.int32)
    return slot_line[None, :] < (grid_shapes[:, 0] * grid_shapes[:, 1])[:, None]

def normalize(values):
    center = lax.optimization_barrier(jnp.mean(values, axis=-1, keepdims=True))
    spread = lax.optimization_barrier(jnp.mean(values * values, axis=-1, keepdims=True)) - center * center
    return (values - center) * lax.rsqrt(spread + EPSILON)

def block(tokens, condition, modulation_weight, modulation_bias, attend_weight, attend_bias, merge_weight, merge_bias, expand_weight, expand_bias, reduce_weight, reduce_bias, position, present):
    images = condition.shape[0]
    lifted = low(jax.nn.silu(condition))
    modulation = low_back(jnp.dot(lifted, modulation_weight.reshape(D, 6 * D), precision=HIGHEST).reshape(images, 6, D) + modulation_bias)
    residual = tokens.reshape(images, SLOTS, D) + position
    features_a = low(normalize(residual) * (1.0 + modulation[:, 1, None, :]) + modulation[:, 0, None, :])
    projected = jnp.einsum('isd,dtf->istf', features_a, attend_weight, precision=HIGHEST)
    queries = low(low_back(projected[:, :, 0] + attend_bias[0])).reshape(images, SLOTS, H, HD)
    keys_side = low(low_back(projected[:, :, 1])).reshape(images, SLOTS, H, HD)
    values_side = low(low_back(projected[:, :, 2] + attend_bias[1])).reshape(images, SLOTS, H, HD)
    scores = low_back(jnp.einsum('iqhe,ikhe->ihqk', queries, keys_side, precision=HIGHEST) * (1.0 / math.sqrt(HD)))
    scores = jnp.where(present[:, None, None, :], scores, NEGATIVE)
    attention = jax.nn.softmax(scores, axis=-1)
    mixture = low(low_back(jnp.einsum('ihqk,ikhe->iqhe', low(attention), values_side, precision=HIGHEST))).reshape(images, SLOTS, H * HD)
    attended = low_back(jnp.einsum('isf,fd->isd', mixture, merge_weight, precision=HIGHEST) + merge_bias)
    middle = residual + modulation[:, 2, None, :] * attended
    features_b = low(normalize(middle) * (1.0 + modulation[:, 4, None, :]) + modulation[:, 3, None, :])
    expanded = low_back(jnp.einsum('isd,df->isf', features_b, expand_weight, precision=HIGHEST) + expand_bias)
    activated = low(jax.nn.gelu(expanded, approximate=True))
    reduced = low_back(jnp.einsum('isf,fd->isd', activated, reduce_weight, precision=HIGHEST) + reduce_bias)
    return (middle + modulation[:, 5, None, :] * reduced).reshape(images * SLOTS, D)

def reference(tokens, condition, grid_shapes, cotangent, modulation_weight, modulation_bias, attend_weight, attend_bias, merge_weight, merge_bias, expand_weight, expand_bias, reduce_weight, reduce_bias):
    params = tuple((weight.astype(jnp.float32) for weight in (modulation_weight, modulation_bias, attend_weight, attend_bias, merge_weight, merge_bias, expand_weight, expand_bias, reduce_weight, reduce_bias)))
    group_size = math.gcd(IMAGES, 8)
    rounds = IMAGES // group_size
    token_blocks = tokens.astype(jnp.float32).T.reshape(rounds, group_size * SLOTS, D)
    cond_blocks = condition.astype(jnp.float32).reshape(rounds, group_size, D)
    grid_blocks = grid_shapes.reshape(rounds, group_size, 2)
    back_blocks = cotangent.astype(jnp.float32).T.reshape(rounds, group_size * SLOTS, D)

    def visit(totals, blocks_in):
        token_part, cond_part, grid_part, back_part = blocks_in
        position = position_table(grid_part, 0, D)
        present = slot_present(grid_part)

        def forward(token_in, cond_in, *weights):
            return block(token_in, cond_in, *weights, position, present)
        result, pullback = jax.vjp(forward, token_part, cond_part, *params)
        pulled = pullback(back_part)
        totals = tuple((total + piece for total, piece in zip(totals, pulled[2:])))
        return (totals, (result, pulled[0], pulled[1]))
    starts = tuple((jnp.zeros_like(weight) for weight in params))
    totals, outs_all = lax.scan(visit, starts, (token_blocks, cond_blocks, grid_blocks, back_blocks))
    results, token_grads, cond_grads = outs_all
    return (results.reshape(TOKENS, D).T, token_grads.reshape(TOKENS, D).T, cond_grads.reshape(IMAGES, D), totals[0], totals[1], totals[2], totals[3], totals[4], totals[5], totals[6], totals[7], totals[8], totals[9])
```

```python
import functools
import math

import jax
import jax.numpy as jnp
from jax import lax
from jax.experimental import pallas as pl
from jax.experimental.pallas import tpu as pltpu
from jax.sharding import PartitionSpec as P

D = 1152
HD = 72
SLOTS = 256
EPSILON = 1e-06
NEGATIVE = -1e30
SPOTS = 64
SCALE = 1.0 / math.sqrt(HD)
F32 = jnp.float32
BF16 = jnp.bfloat16


def times(left, right, dim_left, dim_right):
    return lax.dot_general(
        left, right, (((dim_left,), (dim_right,)), ((), ())), preferred_element_type=F32
    )


def gelu_tanh(values):
    return jax.nn.gelu(values, approximate=True)


ARB = pltpu.CompilerParams(dimension_semantics=("arbitrary",))


def smem():
    return pl.BlockSpec(memory_space=pltpu.SMEM)


def image_rows(count, width):
    return pl.BlockSpec((count, width, SLOTS), lambda i: (0, 0, i))


def column_spec(width):
    return pl.BlockSpec((1, D, width), lambda i: (i, 0, 0))


def rows_of(ref, i, blk):
    return slice(i * blk, (i + 1) * blk)


def cost(flops, moved, trans=0):
    return pl.CostEstimate(flops=flops, bytes_accessed=moved, transcendentals=trans)


def pre_kernel(idx, tokens, table, spots, mod, res, feat, stats):
    count, blk, _ = tokens.shape
    line = lax.broadcasted_iota(jnp.int32, (6 * SPOTS, SLOTS), 0)
    target = jnp.where(line < 3 * SPOTS, spots[0, 0:1, :], spots[0, 1:2, :])
    onehot = jnp.where((line & (SPOTS - 1)) == target, 1.0, 0.0).astype(BF16)
    total = jnp.zeros((1, SLOTS), F32)
    square = jnp.zeros((1, SLOTS), F32)
    for i in range(count):
        value = tokens[idx[i]].astype(F32) + times(table[i], onehot, 1, 0)
        res[i] = value
        total = total + jnp.sum(value, axis=0, keepdims=True)
        square = square + jnp.sum(value * value, axis=0, keepdims=True)
    center = total * (1.0 / D)
    factor = lax.rsqrt(square * (1.0 / D) - center * center + EPSILON)
    stats[0:1, :] = center
    stats[1:2, :] = factor
    for i in range(count):
        rows = slice(i * blk, (i + 1) * blk)
        normed = (res[i] - center) * factor
        feat[i] = (normed * (1.0 + mod[0, rows, 1:2]) + mod[0, rows, 0:1]).astype(BF16)


def mid_kernel(res, att, mod, mid, feat, stats):
    count, blk, _ = res.shape
    total = jnp.zeros((1, SLOTS), F32)
    square = jnp.zeros((1, SLOTS), F32)
    for i in range(count):
        rows = slice(i * blk, (i + 1) * blk)
        value = res[i] + mod[0, rows, 2:3] * att[i]
        mid[i] = value
        total = total + jnp.sum(value, axis=0, keepdims=True)
        square = square + jnp.sum(value * value, axis=0, keepdims=True)
    center = total * (1.0 / D)
    factor = lax.rsqrt(square * (1.0 / D) - center * center + EPSILON)
    stats[0:1, :] = center
    stats[1:2, :] = factor
    for i in range(count):
        rows = slice(i * blk, (i + 1) * blk)
        normed = (mid[i] - center) * factor
        feat[i] = (normed * (1.0 + mod[0, rows, 4:5]) + mod[0, rows, 3:4]).astype(BF16)


def out_kernel(idx, mid, red, cot, mod, own, other, red_grad, cols, hold):
    count, blk, _ = mid.shape
    for i in range(count):
        rows = slice(i * blk, (i + 1) * blk)
        gate = mod[0, rows, 5:6]
        reduced = red[i]
        upstream = cot[idx[i]].astype(F32)
        hold[idx[i]] = mid[i] + gate * reduced
        rounded = (upstream * gate).astype(BF16)
        red_grad[i] = rounded
        cols[0, rows, 0:1] = jnp.sum(upstream * reduced, axis=1, keepdims=True)
        cols[0, rows, 1:2] = jnp.sum(rounded.astype(F32), axis=1, keepdims=True)
    kept = own.shape[0]
    own[...] = hold[0:kept]
    if other is not None:
        other[...] = hold[kept:count].astype(other.dtype)


def back_mid_kernel(idx, fgrad, mid, stats, mod, cot, att, mid_grad, att_grad, cols):
    count, blk, _ = mid.shape
    center, factor = stats[0:1, :], stats[1:2, :]
    first = jnp.zeros((1, SLOTS), F32)
    second = jnp.zeros((1, SLOTS), F32)
    for i in range(count):
        rows = slice(i * blk, (i + 1) * blk)
        grad = fgrad[i]
        normed = (mid[i] - center) * factor
        both = grad * normed
        scale = 1.0 + mod[0, rows, 4:5]
        cols[0, rows, 0:1] = jnp.sum(grad, axis=1, keepdims=True)
        cols[0, rows, 1:2] = jnp.sum(both, axis=1, keepdims=True)
        first = first + jnp.sum(grad * scale, axis=0, keepdims=True)
        second = second + jnp.sum(both * scale, axis=0, keepdims=True)
    first = first * (1.0 / D)
    second = second * (1.0 / D)
    for i in range(count):
        rows = slice(i * blk, (i + 1) * blk)
        scale = 1.0 + mod[0, rows, 4:5]
        normed = (mid[i] - center) * factor
        value = cot[idx[i]].astype(F32) + factor * (fgrad[i] * scale - first - normed * second)
        mid_grad[i] = value
        rounded = (value * mod[0, rows, 2:3]).astype(BF16)
        att_grad[i] = rounded
        cols[0, rows, 2:3] = jnp.sum(value * att[i], axis=1, keepdims=True)
        cols[0, rows, 3:4] = jnp.sum(rounded.astype(F32), axis=1, keepdims=True)


def back_pre_kernel(idx, fgrad, res, stats, mod, mid_grad, own, other, cols, hold):
    count, blk, _ = res.shape
    center, factor = stats[0:1, :], stats[1:2, :]
    first = jnp.zeros((1, SLOTS), F32)
    second = jnp.zeros((1, SLOTS), F32)
    for i in range(count):
        rows = slice(i * blk, (i + 1) * blk)
        grad = fgrad[i]
        normed = (res[i] - center) * factor
        both = grad * normed
        scale = 1.0 + mod[0, rows, 1:2]
        cols[0, rows, 0:1] = jnp.sum(grad, axis=1, keepdims=True)
        cols[0, rows, 1:2] = jnp.sum(both, axis=1, keepdims=True)
        first = first + jnp.sum(grad * scale, axis=0, keepdims=True)
        second = second + jnp.sum(both * scale, axis=0, keepdims=True)
    first = first * (1.0 / D)
    second = second * (1.0 / D)
    for i in range(count):
        rows = slice(i * blk, (i + 1) * blk)
        scale = 1.0 + mod[0, rows, 1:2]
        normed = (res[i] - center) * factor
        hold[idx[i]] = mid_grad[i] + factor * (fgrad[i] * scale - first - normed * second)
    kept = own.shape[0]
    own[...] = hold[0:kept]
    if other is not None:
        other[...] = hold[kept:count].astype(other.dtype)


def masked_scores(keys, queries, present):
    raw = times(keys, queries, 0, 0) * SCALE
    slot = lax.broadcasted_iota(jnp.int32, raw.shape, 0)
    return jnp.where(slot < present, raw, NEGATIVE)


def attend_kernel(present, qkv, mix, logs):
    here = present[pl.program_id(0)]
    for h in range(mix.shape[0]):
        scores = masked_scores(qkv[1, h], qkv[0, h], here)
        highest = jnp.max(scores, axis=0, keepdims=True)
        weight = jnp.exp(scores - highest)
        total = jnp.sum(weight, axis=0, keepdims=True)
        logs[h : h + 1, :] = highest + jnp.log(total)
        attention = (weight * (1.0 / total)).astype(BF16)
        mix[h] = times(qkv[2, h], attention, 1, 0).astype(BF16)


def attend_back_kernel(present, qkv, mix_grad, logs, grads):
    here = present[pl.program_id(0)]
    for h in range(mix_grad.shape[0]):
        queries, keys, values, upstream = qkv[0, h], qkv[1, h], qkv[2, h], mix_grad[h]
        attention = jnp.exp(masked_scores(keys, queries, here) - logs[h : h + 1, :])
        att_grad = times(values, upstream, 0, 0)
        inner = jnp.sum(attention * att_grad, axis=0, keepdims=True)
        score_grad = (attention * (att_grad - inner)).astype(BF16)
        grads[0, h] = (times(keys, score_grad, 1, 0) * SCALE).astype(BF16)
        grads[1, h] = (times(queries, score_grad, 1, 1) * SCALE).astype(BF16)
        grads[2, h] = times(upstream, attention.astype(BF16), 1, 1).astype(BF16)


def build(mesh):
    FS, T = mesh.shape["fsdp"], mesh.shape["tensor"]
    staged = T == 2 and FS % 8 == 0 and (D // FS) % 8 == 0
    Z = FS // 4
    swap_x = [(0, 1), (1, 0)]
    swap_y = [(i, i ^ 2) for i in range(FS)]
    swap_c = [(i, i ^ 1) for i in range(FS)]
    ring_z = [(i, (i + 4) % FS) for i in range(FS)]

    def over_x(v):
        return lax.ppermute(v, "tensor", swap_x)

    def over_y(v):
        return lax.ppermute(v, "fsdp", swap_y)

    def over_c(v):
        return lax.ppermute(v, "fsdp", swap_c)

    def over_z(v):
        return lax.ppermute(v, "fsdp", ring_z)

    def gather_weights(piece):
        if not staged:
            whole = lax.all_gather(piece, "fsdp", axis=0, tiled=True)
            whole = lax.all_gather(whole, "tensor", axis=0, tiled=False)
            return [[whole[i]] for i in range(T)]
        held = [piece]
        for _ in range(Z - 1):
            held.append(over_z(held[-1]))
        base = jnp.concatenate(held, axis=0)
        half = base.shape[0] // 2
        side_x, side_y = over_x(base), over_y(base)
        far_a = over_x(side_y[:half])
        far_b = over_y(side_x[half:])
        own = [base, side_y]
        other = [side_x, far_a, far_b]
        own = own + [over_c(v) for v in own]
        other = other + [over_c(v) for v in other]
        return [own, other]

    def joined(parts, start, stop):
        return jnp.concatenate([v[:, start:stop] for v in parts], axis=0)

    def scatter_grads(left, rights):
        if not staged:
            local = jnp.stack([times(left, r, 1, 1).astype(BF16) for r in rights], axis=0)
            part = lax.psum_scatter(local, "tensor", scatter_dimension=0, tiled=True)[0]
            return lax.psum_scatter(part, "fsdp", scatter_dimension=0, tiled=True).astype(F32)
        rows = D // 2
        sent = [over_c(times(left[rows:], r, 1, 1).astype(BF16)) for r in rights]
        own, other = [
            (times(left[:rows], r, 1, 1) + s.astype(F32)).astype(BF16)
            for r, s in zip(rights, sent)
        ]
        quarter, half = rows // 4, rows // 2
        from_x = over_x(other[half : half + quarter]).astype(F32)
        from_y = over_y(other[half + quarter :]).astype(F32)
        send_y = jnp.concatenate(
            [
                (own[half : half + quarter].astype(F32) + from_x).astype(BF16),
                own[half + quarter :],
            ],
            axis=0,
        )
        send_x = jnp.concatenate(
            [
                other[:quarter],
                (other[quarter:half].astype(F32) + from_y).astype(BF16),
            ],
            axis=0,
        )
        base = own[:half].astype(F32) + over_x(send_x).astype(F32) + over_y(send_y).astype(F32)
        blk = half // Z
        moving = base[blk : 2 * blk].astype(BF16)
        for k in range(2, Z + 1):
            slot = k % Z
            moving = over_z(moving).astype(F32) + base[slot * blk : (slot + 1) * blk]
            if slot:
                moving = moving.astype(BF16)
        return moving

    def per_device(
        tokens,
        condition,
        grid_shapes,
        cotangent,
        modulation_weight,
        modulation_bias,
        attend_weight,
        attend_bias,
        merge_weight,
        merge_bias,
        expand_weight,
        expand_bias,
        reduce_weight,
        reduce_bias,
    ):
        width = tokens.shape[0]
        hidden = expand_weight.shape[1]
        heads = width // HD
        group = condition.shape[0]
        images = group // T
        tok = images * SLOTS
        t, f = lax.axis_index("tensor"), lax.axis_index("fsdp")
        NB = FS if staged else 16
        blk = D // NB
        KB = NB // T if staged else NB
        rows_w = D // FS

        slot = jnp.arange(NB, dtype=jnp.int32)
        if staged:
            z, y, c = f // 4, (f // 2) % 2, f % 2
            c_rel, y_rel, k_rel = slot // (2 * Z), (slot // Z) % 2, slot % Z
            order = ((z - k_rel + Z) % Z) * 4 + (y ^ y_rel) * 2 + (c ^ c_rel)
            pick = ((order // KB) ^ t) * KB + order % KB
        else:
            order = slot
            pick = slot
        back = jnp.sum(
            jnp.where(pick[None, :] == slot[:, None], slot[None, :], 0), axis=1
        )

        attend_parts = gather_weights(attend_weight.reshape(rows_w, 3 * width))
        second_parts = gather_weights(
            jnp.concatenate([merge_weight.T, expand_weight], axis=1)
        )
        reduce_parts = gather_weights(reduce_weight.T)

        def spread(array):
            if not staged:
                whole = lax.all_to_all(array, "tensor", split_axis=1, concat_axis=0, tiled=True)
                return whole.reshape(NB, blk, tok)
            own = lax.dynamic_slice(array, (0, t * tok), (width, tok))
            recv = over_x(lax.dynamic_slice(array, (0, (1 - t) * tok), (width, tok)))
            return jnp.concatenate([own, recv], axis=0).reshape(NB, blk, tok)

        def collect(own, other):
            if not staged:
                return lax.all_to_all(
                    own.reshape(D, tok), "tensor", split_axis=0, concat_axis=1, tiled=True
                )
            recv = over_x(other).astype(F32).reshape(width, tok)
            own = own.reshape(width, tok)
            first = jnp.where(t == 0, own, recv)
            last = jnp.where(t == 0, recv, own)
            return jnp.concatenate([first, last], axis=1)

        cond = condition.astype(F32)
        lifted = jax.nn.silu(cond).astype(BF16)
        lifted_all = lax.all_gather(lifted, "fsdp", axis=0, tiled=True)
        lifted_cols = lax.dynamic_slice(
            lifted_all, (0, f * rows_w), (lifted_all.shape[0], rows_w)
        )
        mod_weight = modulation_weight.reshape(rows_w, 6 * width)
        mod_part = times(lifted_cols, mod_weight, 1, 0)
        mod_group = lax.psum_scatter(mod_part, "fsdp", scatter_dimension=0, tiled=True)
        mod_group = mod_group.reshape(group, 6, width) + modulation_bias.astype(F32)
        if staged:
            own = lax.dynamic_slice(mod_group, (t * images, 0, 0), (images, 6, width))
            recv = over_x(
                lax.dynamic_slice(mod_group, ((1 - t) * images, 0, 0), (images, 6, width))
            )
            mod = jnp.concatenate([own, recv], axis=2)
        else:
            mod = lax.all_to_all(mod_group, "tensor", split_axis=0, concat_axis=2, tiled=True)
        mod = jnp.take(mod.reshape(images, 6, NB, blk), pick, axis=2).reshape(images, 6, D)
        mod = jnp.pad(jnp.swapaxes(mod, 1, 2), ((0, 0), (0, 0), (0, 2)))

        bias_local = jnp.concatenate(
            [attend_bias.reshape(-1), expand_bias, merge_bias, reduce_bias]
        )
        if staged:
            bias_all = jnp.stack([bias_local, over_x(bias_local)], axis=0)
        else:
            bias_all = lax.all_gather(bias_local, "tensor", axis=0, tiled=False)
        bias_all = bias_all.astype(F32)
        at = 2 * width
        zeros = jnp.zeros((T, width), F32)
        attend_b = jnp.concatenate([bias_all[:, :width], zeros, bias_all[:, width:at]], axis=1)
        expand_b = bias_all[:, at : at + hidden]
        at = at + hidden

        def channels(block):
            return jnp.take(block.reshape(NB, blk), pick, axis=0).reshape(D, 1)

        merge_b = channels(bias_all[:, at : at + width])
        reduce_b = channels(bias_all[:, at + width : at + 2 * width])

        grids = lax.dynamic_slice(grid_shapes, (t * images, 0), (images, 2))
        present = grids[:, 0] * grids[:, 1]
        line = jnp.arange(SLOTS, dtype=jnp.int32)
        spots = jnp.stack([line[None, :] // grids[:, 1:2], line[None, :] % grids[:, 1:2]], axis=1)
        spots = jnp.pad(spots, ((0, 0), (0, 6), (0, 0)))
        channel = (order[:, None] * blk + jnp.arange(blk, dtype=jnp.int32)[None, :]).reshape(D)
        quarter = channel // (D // 4)
        within = channel % (D // 4)
        frequency = jnp.exp(within.astype(F32) * (-math.log(10000.0) / (D // 4)))
        angle = jnp.arange(SPOTS, dtype=jnp.int32).astype(F32)[None, :] * frequency[:, None]
        wave = jnp.where((quarter % 2 == 0)[:, None], jnp.sin(angle), jnp.cos(angle))
        high = lax.reduce_precision(wave, 8, 7)
        middle_bits = lax.reduce_precision(wave - high, 8, 7)
        low_bits = lax.reduce_precision(wave - high - middle_bits, 8, 7)
        bits = jnp.concatenate([high, middle_bits, low_bits], axis=1)
        by_row = (quarter < 2)[:, None]
        table = jnp.concatenate(
            [jnp.where(by_row, bits, 0.0), jnp.where(by_row, 0.0, bits)], axis=1
        )
        table = table.astype(BF16).reshape(NB, blk, 6 * SPOTS)

        cube = (NB, blk, tok)
        big = image_rows(NB, blk)
        kept_spec = image_rows(KB, blk)
        stat_spec = pl.BlockSpec((8, SLOTS), lambda i: (0, i))
        act_bytes = D * tok * 4

        tokens_all = spread(tokens)
        cot_all = spread(cotangent)
        residual, features_a, stats_a = pl.pallas_call(
            pre_kernel,
            name="pre",
            grid=(images,),
            in_specs=[
                smem(),
                big,
                pl.BlockSpec((NB, blk, 6 * SPOTS), lambda i: (0, 0, 0)),
                pl.BlockSpec((1, 8, SLOTS), lambda i: (i, 0, 0)),
                column_spec(8),
            ],
            out_specs=[big, big, stat_spec],
            out_shape=[
                jax.ShapeDtypeStruct(cube, F32),
                jax.ShapeDtypeStruct(cube, BF16),
                jax.ShapeDtypeStruct((8, tok), F32),
            ],
            compiler_params=ARB,
            cost_estimate=cost(2 * D * tok * 384, 2 * act_bytes),
        )(pick, tokens_all, table, spots, mod)
        features_a = features_a.reshape(D, tok)

        attend_w = [joined(p, 0, 3 * width) for p in attend_parts]
        head_cube = (heads, HD, tok)
        qkv_spec = pl.BlockSpec((3, heads, HD, SLOTS), lambda i: (0, 0, 0, i))
        head_spec = pl.BlockSpec((heads, HD, SLOTS), lambda i: (0, 0, i))
        log_spec = pl.BlockSpec((heads, SLOTS), lambda i: (0, i))
        qkv, mixture, logs = [], [], []
        for i in range(T):
            projected = times(attend_w[i], features_a, 0, 0) + attend_b[i][:, None]
            qkv.append(projected.astype(BF16).reshape(3, heads, HD, tok))
            mix, log = pl.pallas_call(
                attend_kernel,
                name="attend",
                grid=(images,),
                in_specs=[smem(), qkv_spec],
                out_specs=[head_spec, log_spec],
                out_shape=[
                    jax.ShapeDtypeStruct(head_cube, BF16),
                    jax.ShapeDtypeStruct((heads, tok), F32),
                ],
                compiler_params=ARB,
                cost_estimate=cost(
                    8 * heads * tok * SLOTS * SLOTS, 8 * width * tok, heads * tok * SLOTS
                ),
            )(present, qkv[i])
            mixture.append(mix.reshape(width, tok))
            logs.append(log)
        merge_w = [joined(p, 0, width) for p in second_parts]
        attended = merge_b + sum(times(merge_w[i], mixture[i], 1, 0) for i in range(T))
        attended = attended.reshape(cube)
        middle, features_b, stats_b = pl.pallas_call(
            mid_kernel,
            name="mid",
            grid=(images,),
            in_specs=[big, big, column_spec(8)],
            out_specs=[big, big, stat_spec],
            out_shape=[
                jax.ShapeDtypeStruct(cube, F32),
                jax.ShapeDtypeStruct(cube, BF16),
                jax.ShapeDtypeStruct((8, tok), F32),
            ],
            compiler_params=ARB,
            cost_estimate=cost(10 * D * tok, 4 * act_bytes),
        )(residual, attended, mod)
        features_b = features_b.reshape(D, tok)

        expand_w = [joined(p, width, width + hidden) for p in second_parts]
        expanded = [times(expand_w[i], features_b, 0, 0) + expand_b[i][:, None] for i in range(T)]
        activated = [gelu_tanh(v).astype(BF16) for v in expanded]
        reduce_w = [joined(p, 0, hidden) for p in reduce_parts]
        reduced = reduce_b + sum(times(reduce_w[i], activated[i], 1, 0) for i in range(T))
        kept_cube = (KB, blk, tok)
        other_specs = [kept_spec] if staged else []
        own_out, *other_out, red_grad, cols_out = pl.pallas_call(
            out_kernel if staged else functools.partial(without_other, out_kernel, 6),
            name="out",
            grid=(images,),
            in_specs=[smem(), big, big, big, column_spec(8)],
            out_specs=[kept_spec, *other_specs, big, column_spec(2)],
            out_shape=[
                jax.ShapeDtypeStruct(kept_cube, F32),
                *[jax.ShapeDtypeStruct(kept_cube, F32) for _ in other_specs],
                jax.ShapeDtypeStruct(cube, BF16),
                jax.ShapeDtypeStruct((images, D, 2), F32),
            ],
            scratch_shapes=[pltpu.VMEM((NB, blk, SLOTS), F32)],
            compiler_params=ARB,
            cost_estimate=cost(10 * D * tok, 4 * act_bytes),
        )(pick, middle, reduced.reshape(cube), cot_all, mod)
        output = collect(own_out, other_out[0] if staged else None)
        red_grad = red_grad.reshape(D, tok)

        expand_grad = [
            jax.vjp(gelu_tanh, expanded[i])[1](times(reduce_w[i], red_grad, 0, 0))[0].astype(BF16)
            for i in range(T)
        ]
        reduce_wg = scatter_grads(red_grad, activated)
        features_b_grad = sum(times(expand_w[i], expand_grad[i], 1, 0) for i in range(T))
        expand_wg = scatter_grads(features_b, expand_grad)
        mid_grad, att_grad, cols_mid = pl.pallas_call(
            back_mid_kernel,
            name="back_mid",
            grid=(images,),
            in_specs=[smem(), big, big, stat_spec, column_spec(8), big, big],
            out_specs=[big, big, column_spec(4)],
            out_shape=[
                jax.ShapeDtypeStruct(cube, F32),
                jax.ShapeDtypeStruct(cube, BF16),
                jax.ShapeDtypeStruct((images, D, 4), F32),
            ],
            compiler_params=ARB,
            cost_estimate=cost(20 * D * tok, 5 * act_bytes),
        )(pick, features_b_grad.reshape(cube), middle, stats_b, mod, cot_all, attended)
        att_grad = att_grad.reshape(D, tok)

        qkv_grad = []
        for i in range(T):
            mix_grad = times(merge_w[i], att_grad, 0, 0).astype(BF16).reshape(head_cube)
            grads = pl.pallas_call(
                attend_back_kernel,
                name="attend_back",
                grid=(images,),
                in_specs=[smem(), qkv_spec, head_spec, log_spec],
                out_specs=qkv_spec,
                out_shape=jax.ShapeDtypeStruct((3, heads, HD, tok), BF16),
                compiler_params=ARB,
                cost_estimate=cost(
                    20 * heads * tok * SLOTS * SLOTS, 16 * width * tok, heads * tok * SLOTS
                ),
            )(present, qkv[i], mix_grad, logs[i])
            qkv_grad.append(grads.reshape(3 * width, tok))
        merge_wg = scatter_grads(att_grad, mixture)
        attend_wg = scatter_grads(features_a, qkv_grad)
        features_a_grad = sum(times(attend_w[i], qkv_grad[i], 1, 0) for i in range(T))
        own_in, *other_in, cols_pre = pl.pallas_call(
            back_pre_kernel if staged else functools.partial(without_other, back_pre_kernel, 7),
            name="back_pre",
            grid=(images,),
            in_specs=[smem(), big, big, stat_spec, column_spec(8), big],
            out_specs=[kept_spec, *other_specs, column_spec(2)],
            out_shape=[
                jax.ShapeDtypeStruct(kept_cube, F32),
                *[jax.ShapeDtypeStruct(kept_cube, BF16) for _ in other_specs],
                jax.ShapeDtypeStruct((images, D, 2), F32),
            ],
            scratch_shapes=[pltpu.VMEM((NB, blk, SLOTS), F32)],
            compiler_params=ARB,
            cost_estimate=cost(20 * D * tok, 5 * act_bytes),
        )(pick, features_a_grad.reshape(cube), residual, stats_a, mod, mid_grad)
        tokens_grad = collect(own_in, other_in[0] if staged else None)

        def own_first(values):
            lead = values.shape[:-1]
            blocks = jnp.take(values.reshape(*lead, NB, blk), back, axis=len(lead))
            return blocks.reshape(*lead, T, width)

        def slot_sums(values):
            return jnp.sum(values.astype(F32), axis=1)

        qkv_sums = [slot_sums(v) for v in qkv_grad]
        hidden_sums = [slot_sums(v) for v in expand_grad]
        merge_sums = own_first(jnp.sum(cols_mid[:, :, 3], axis=0))
        reduce_sums = own_first(jnp.sum(cols_out[:, :, 1], axis=0))
        bias_rows = [
            jnp.concatenate(
                [
                    qkv_sums[i][:width],
                    qkv_sums[i][2 * width :],
                    merge_sums[i],
                    hidden_sums[i],
                    reduce_sums[i],
                ]
            )
            for i in range(T)
        ]
        if staged:
            bias_sum = bias_rows[0] + over_x(bias_rows[1])
        else:
            bias_sum = lax.psum_scatter(
                jnp.stack(bias_rows), "tensor", scatter_dimension=0, tiled=True
            )[0]
        bias_sum = lax.psum(bias_sum, "fsdp")

        mod_grad = jnp.stack(
            [
                cols_pre[:, :, 0],
                cols_pre[:, :, 1],
                cols_mid[:, :, 2],
                cols_mid[:, :, 0],
                cols_mid[:, :, 1],
                cols_out[:, :, 0],
            ],
            axis=1,
        ).astype(BF16)
        mod_grad = own_first(mod_grad)
        if staged:
            mine, recv = mod_grad[:, :, 0], over_x(mod_grad[:, :, 1])
            mod_grad = jnp.concatenate(
                [jnp.where(t == 0, mine, recv), jnp.where(t == 0, recv, mine)], axis=0
            )
        else:
            mod_grad = lax.all_to_all(
                mod_grad, "tensor", split_axis=2, concat_axis=0, tiled=True
            )
        flat_grad = mod_grad.reshape(group, 6 * width)
        flat_all = lax.all_gather(flat_grad, "fsdp", axis=0, tiled=True)
        mod_wg = times(lifted_cols, flat_all, 0, 0).reshape(rows_w, 6, width)
        mod_bg = jnp.sum(flat_all.astype(F32), axis=0).reshape(6, width)
        lift_part = times(flat_all, mod_weight, 1, 1)
        lift_rows = lax.all_to_all(lift_part, "fsdp", split_axis=0, concat_axis=1, tiled=True)
        if staged:
            lift_mine = lax.dynamic_slice(lift_rows, (0, t * width), (group, width))
            lift_sent = lax.dynamic_slice(lift_rows, (0, (1 - t) * width), (group, width))
            lift_grad = lift_mine + over_x(lift_sent)
        else:
            lift_grad = lax.psum_scatter(lift_rows, "tensor", scatter_dimension=1, tiled=True)
        cond_here = lax.dynamic_slice(cond, (0, t * width), (group, width))
        cond_grad = jax.vjp(jax.nn.silu, cond_here)[1](lift_grad)[0]

        bounds = [0, 2 * width, 3 * width, 3 * width + hidden, 4 * width + hidden]
        attend_bg, merge_bg, expand_bg, reduce_bg = [
            bias_sum[a:b] for a, b in zip(bounds[:-1], bounds[1:])
        ]
        return (
            output,
            tokens_grad,
            cond_grad,
            mod_wg,
            mod_bg,
            attend_wg.reshape(rows_w, 3, width),
            attend_bg.reshape(2, width),
            merge_wg.T,
            merge_bg,
            expand_wg,
            expand_bg,
            reduce_wg.T,
            reduce_bg,
        )

    return per_device


def without_other(body, place, *refs):
    return body(*refs[:place], None, *refs[place:])


def solution(mesh):
    return jax.shard_map(
        build(mesh),
        mesh=mesh,
        in_specs=(
            P("tensor", "fsdp"),
            P("fsdp", None),
            P("fsdp", None),
            P("tensor", "fsdp"),
            P("fsdp", None, "tensor"),
            P(None, "tensor"),
            P("fsdp", None, "tensor"),
            P(None, "tensor"),
            P("tensor", "fsdp"),
            P("tensor"),
            P("fsdp", "tensor"),
            P("tensor"),
            P("tensor", "fsdp"),
            P("tensor"),
        ),
        out_specs=(
            P("tensor", "fsdp"),
            P("tensor", "fsdp"),
            P("fsdp", "tensor"),
            P("fsdp", None, "tensor"),
            P(None, "tensor"),
            P("fsdp", None, "tensor"),
            P(None, "tensor"),
            P("tensor", "fsdp"),
            P("tensor"),
            P("fsdp", "tensor"),
            P("tensor"),
            P("tensor", "fsdp"),
            P("tensor"),
        ),
        check_vma=False,
    )
```

```python
import functools
import math

import jax
import jax.numpy as jnp
from jax import lax
from jax.experimental import pallas as pl
from jax.experimental.pallas import tpu as pltpu
from jax.sharding import PartitionSpec as P

D = 1152
HD = 72
SLOTS = 256
EPSILON = 1e-06
NEGATIVE = -1e30
SPOTS = 64
SCALE = 1.0 / math.sqrt(HD)
F32 = jnp.float32
BF16 = jnp.bfloat16


def times(left, right, dim_left, dim_right):
    return lax.dot_general(
        left, right, (((dim_left,), (dim_right,)), ((), ())), preferred_element_type=F32
    )


def fence(*trees):
    return lax.optimization_barrier(trees)


def gelu_tanh(values):
    return jax.nn.gelu(values, approximate=True)


ARB = pltpu.CompilerParams(dimension_semantics=("arbitrary",))


def smem():
    return pl.BlockSpec(memory_space=pltpu.SMEM)


def image_rows(count, width):
    return pl.BlockSpec((count, width, SLOTS), lambda i: (0, 0, i))


def column_spec(width):
    return pl.BlockSpec((1, D, width), lambda i: (i, 0, 0))


def rows_of(ref, i, blk):
    return slice(i * blk, (i + 1) * blk)


def cost(flops, moved, trans=0):
    return pl.CostEstimate(flops=flops, bytes_accessed=moved, transcendentals=trans)


def pre_kernel(idx, tokens, table, spots, mod, res, feat, stats):
    count, blk, _ = tokens.shape
    line = lax.broadcasted_iota(jnp.int32, (6 * SPOTS, SLOTS), 0)
    target = jnp.where(line < 3 * SPOTS, spots[0, 0:1, :], spots[0, 1:2, :])
    onehot = jnp.where((line & (SPOTS - 1)) == target, 1.0, 0.0).astype(BF16)
    total = jnp.zeros((1, SLOTS), F32)
    square = jnp.zeros((1, SLOTS), F32)
    for i in range(count):
        value = tokens[idx[i]].astype(F32) + times(table[i], onehot, 1, 0)
        res[i] = value
        total = total + jnp.sum(value, axis=0, keepdims=True)
        square = square + jnp.sum(value * value, axis=0, keepdims=True)
    center = total * (1.0 / D)
    factor = lax.rsqrt(square * (1.0 / D) - center * center + EPSILON)
    stats[0:1, :] = center
    stats[1:2, :] = factor
    for i in range(count):
        rows = slice(i * blk, (i + 1) * blk)
        normed = (res[i] - center) * factor
        feat[i] = (normed * (1.0 + mod[0, rows, 1:2]) + mod[0, rows, 0:1]).astype(BF16)


def mid_kernel(res, att, mod, mid, feat, stats):
    count, blk, _ = res.shape
    total = jnp.zeros((1, SLOTS), F32)
    square = jnp.zeros((1, SLOTS), F32)
    for i in range(count):
        rows = slice(i * blk, (i + 1) * blk)
        value = res[i] + mod[0, rows, 2:3] * att[i]
        mid[i] = value
        total = total + jnp.sum(value, axis=0, keepdims=True)
        square = square + jnp.sum(value * value, axis=0, keepdims=True)
    center = total * (1.0 / D)
    factor = lax.rsqrt(square * (1.0 / D) - center * center + EPSILON)
    stats[0:1, :] = center
    stats[1:2, :] = factor
    for i in range(count):
        rows = slice(i * blk, (i + 1) * blk)
        normed = (mid[i] - center) * factor
        feat[i] = (normed * (1.0 + mod[0, rows, 4:5]) + mod[0, rows, 3:4]).astype(BF16)


def out_kernel(idx, mid, red, cot, mod, own, other, red_grad, cols, hold):
    count, blk, _ = mid.shape
    for i in range(count):
        rows = slice(i * blk, (i + 1) * blk)
        gate = mod[0, rows, 5:6]
        reduced = red[i]
        upstream = cot[idx[i]].astype(F32)
        hold[idx[i]] = mid[i] + gate * reduced
        rounded = (upstream * gate).astype(BF16)
        red_grad[i] = rounded
        cols[0, rows, 0:1] = jnp.sum(upstream * reduced, axis=1, keepdims=True)
        cols[0, rows, 1:2] = jnp.sum(rounded.astype(F32), axis=1, keepdims=True)
    kept = own.shape[0]
    own[...] = hold[0:kept]
    if other is not None:
        other[...] = hold[kept:count].astype(other.dtype)


def back_mid_kernel(idx, fgrad, mid, stats, mod, cot, att, mid_grad, att_grad, cols):
    count, blk, _ = mid.shape
    center, factor = stats[0:1, :], stats[1:2, :]
    first = jnp.zeros((1, SLOTS), F32)
    second = jnp.zeros((1, SLOTS), F32)
    for i in range(count):
        rows = slice(i * blk, (i + 1) * blk)
        grad = fgrad[i]
        normed = (mid[i] - center) * factor
        both = grad * normed
        scale = 1.0 + mod[0, rows, 4:5]
        cols[0, rows, 0:1] = jnp.sum(grad, axis=1, keepdims=True)
        cols[0, rows, 1:2] = jnp.sum(both, axis=1, keepdims=True)
        first = first + jnp.sum(grad * scale, axis=0, keepdims=True)
        second = second + jnp.sum(both * scale, axis=0, keepdims=True)
    first = first * (1.0 / D)
    second = second * (1.0 / D)
    for i in range(count):
        rows = slice(i * blk, (i + 1) * blk)
        scale = 1.0 + mod[0, rows, 4:5]
        normed = (mid[i] - center) * factor
        value = cot[idx[i]].astype(F32) + factor * (fgrad[i] * scale - first - normed * second)
        mid_grad[i] = value
        rounded = (value * mod[0, rows, 2:3]).astype(BF16)
        att_grad[i] = rounded
        cols[0, rows, 2:3] = jnp.sum(value * att[i], axis=1, keepdims=True)
        cols[0, rows, 3:4] = jnp.sum(rounded.astype(F32), axis=1, keepdims=True)


def back_pre_kernel(idx, fgrad, res, stats, mod, mid_grad, own, other, cols, hold):
    count, blk, _ = res.shape
    center, factor = stats[0:1, :], stats[1:2, :]
    first = jnp.zeros((1, SLOTS), F32)
    second = jnp.zeros((1, SLOTS), F32)
    for i in range(count):
        rows = slice(i * blk, (i + 1) * blk)
        grad = fgrad[i]
        normed = (res[i] - center) * factor
        both = grad * normed
        scale = 1.0 + mod[0, rows, 1:2]
        cols[0, rows, 0:1] = jnp.sum(grad, axis=1, keepdims=True)
        cols[0, rows, 1:2] = jnp.sum(both, axis=1, keepdims=True)
        first = first + jnp.sum(grad * scale, axis=0, keepdims=True)
        second = second + jnp.sum(both * scale, axis=0, keepdims=True)
    first = first * (1.0 / D)
    second = second * (1.0 / D)
    for i in range(count):
        rows = slice(i * blk, (i + 1) * blk)
        scale = 1.0 + mod[0, rows, 1:2]
        normed = (res[i] - center) * factor
        hold[idx[i]] = mid_grad[i] + factor * (fgrad[i] * scale - first - normed * second)
    kept = own.shape[0]
    own[...] = hold[0:kept]
    if other is not None:
        other[...] = hold[kept:count].astype(other.dtype)


def masked_scores(keys, queries, present):
    raw = times(keys, queries, 0, 0) * SCALE
    slot = lax.broadcasted_iota(jnp.int32, raw.shape, 0)
    return jnp.where(slot < present, raw, NEGATIVE)


def attend_kernel(present, qkv, mix, logs):
    here = present[pl.program_id(0)]
    for h in range(mix.shape[0]):
        scores = masked_scores(qkv[1, h], qkv[0, h], here)
        highest = jnp.max(scores, axis=0, keepdims=True)
        weight = jnp.exp(scores - highest)
        total = jnp.sum(weight, axis=0, keepdims=True)
        logs[h : h + 1, :] = highest + jnp.log(total)
        attention = (weight * (1.0 / total)).astype(BF16)
        mix[h] = times(qkv[2, h], attention, 1, 0).astype(BF16)


def attend_back_kernel(present, qkv, mix_grad, logs, grads):
    here = present[pl.program_id(0)]
    for h in range(mix_grad.shape[0]):
        queries, keys, values, upstream = qkv[0, h], qkv[1, h], qkv[2, h], mix_grad[h]
        attention = jnp.exp(masked_scores(keys, queries, here) - logs[h : h + 1, :])
        att_grad = times(values, upstream, 0, 0)
        inner = jnp.sum(attention * att_grad, axis=0, keepdims=True)
        score_grad = (attention * (att_grad - inner)).astype(BF16)
        grads[0, h] = (times(keys, score_grad, 1, 0) * SCALE).astype(BF16)
        grads[1, h] = (times(queries, score_grad, 1, 1) * SCALE).astype(BF16)
        grads[2, h] = times(upstream, attention.astype(BF16), 1, 1).astype(BF16)


def build(mesh):
    FS, T = mesh.shape["fsdp"], mesh.shape["tensor"]
    staged = T == 2 and FS == 16
    Z = FS // 4
    swap_x = [(0, 1), (1, 0)]
    swap_y = [(i, i ^ 2) for i in range(FS)]
    swap_c = [(i, i ^ 1) for i in range(FS)]
    ring_z = [(i, (i + 4) % FS) for i in range(FS)]

    def over_x(v):
        return lax.ppermute(v, "tensor", swap_x)

    def over_y(v):
        return lax.ppermute(v, "fsdp", swap_y)

    def over_c(v):
        return lax.ppermute(v, "fsdp", swap_c)

    def over_z(v):
        return lax.ppermute(v, "fsdp", ring_z)

    def along_z(piece):
        if not staged:
            return piece
        held = [piece]
        for _ in range(Z - 1):
            held.append(over_z(held[-1]))
        return jnp.concatenate(held, axis=0)

    def across(base):
        if not staged:
            whole = lax.all_gather(base, "fsdp", axis=0, tiled=True)
            whole = lax.all_gather(whole, "tensor", axis=0, tiled=False)
            return [[whole[i]] for i in range(T)], whole
        half = base.shape[0] // 2
        side_x, side_y = over_x(base), over_y(base)
        far_a = over_x(side_y[:half])
        far_b = over_y(side_x[half:])
        own = [base, side_y]
        other = [side_x, far_a, far_b]
        last = (far_a, far_b)
        own = own + [over_c(v) for v in own]
        other = other + [over_c(v) for v in other]
        return [own, other], last

    def joined(parts, start, stop):
        return jnp.concatenate([v[:, start:stop] for v in parts], axis=0)

    def all_sum(values):
        if not staged:
            return lax.psum(values, "fsdp")
        bit = 1
        while bit < FS:
            values = values + lax.ppermute(values, "fsdp", [(i, i ^ bit) for i in range(FS)])
            bit *= 2
        return values

    class Scatter:
        def __init__(self, left, rights):
            self.left, self.rights, self.state = left, rights, ()

        def low(self):
            start = D // 2 if staged else 0
            self.state = [times(self.left[start:], r, 1, 1).astype(BF16) for r in self.rights]
            return self

        def core(self):
            if not staged:
                return self
            sent = [over_c(v) for v in self.state]
            self.state = [
                (times(self.left[: D // 2], r, 1, 1) + v.astype(F32)).astype(BF16)
                for r, v in zip(self.rights, sent)
            ]
            return self

        def first(self):
            if not staged:
                return self
            own, other = self.state
            quarter, half = D // 8, D // 4
            from_x = over_x(other[half : half + quarter]).astype(F32)
            from_y = over_y(other[half + quarter :]).astype(F32)
            send_y = [
                (own[half : half + quarter].astype(F32) + from_x).astype(BF16),
                own[half + quarter :],
            ]
            send_x = [
                other[:quarter],
                (other[quarter:half].astype(F32) + from_y).astype(BF16),
            ]
            self.state = [
                own[:half],
                jnp.concatenate(send_x, axis=0),
                jnp.concatenate(send_y, axis=0),
            ]
            return self

        def second(self):
            if not staged:
                return self
            own, send_x, send_y = self.state
            base = own.astype(F32) + over_x(send_x).astype(F32) + over_y(send_y).astype(F32)
            self.state = [base, base[D // 4 // Z : D // 2 // Z].astype(BF16)]
            self.step = 2
            return self

        def ring(self):
            if not staged:
                return self
            base, moving = self.state
            blk = base.shape[0] // Z
            at = self.step % Z
            moving = over_z(moving).astype(F32) + base[at * blk : (at + 1) * blk]
            self.step += 1
            self.state = [base, moving.astype(BF16) if at else moving]
            return self

        def done(self):
            if staged:
                return self.state[1]
            part = lax.psum_scatter(
                jnp.stack(self.state), "tensor", scatter_dimension=0, tiled=True
            )[0]
            return lax.psum_scatter(part, "fsdp", scatter_dimension=0, tiled=True).astype(F32)

    def per_device(
        tokens,
        condition,
        grid_shapes,
        cotangent,
        modulation_weight,
        modulation_bias,
        attend_weight,
        attend_bias,
        merge_weight,
        merge_bias,
        expand_weight,
        expand_bias,
        reduce_weight,
        reduce_bias,
    ):
        width = tokens.shape[0]
        hidden = expand_weight.shape[1]
        heads = width // HD
        group = condition.shape[0]
        images = group // T
        tok = images * SLOTS
        t, f = lax.axis_index("tensor"), lax.axis_index("fsdp")
        NB = FS if staged else 16
        blk = D // NB
        KB = NB // T if staged else NB
        rows_w = D // FS

        slot = jnp.arange(NB, dtype=jnp.int32)
        if staged:
            z, y, c = f // 4, (f // 2) % 2, f % 2
            c_rel, y_rel, k_rel = slot // (2 * Z), (slot // Z) % 2, slot % Z
            order = ((z - k_rel + Z) % Z) * 4 + (y ^ y_rel) * 2 + (c ^ c_rel)
            pick = ((order // KB) ^ t) * KB + order % KB
        else:
            order = slot
            pick = slot
        back = jnp.sum(
            jnp.where(pick[None, :] == slot[:, None], slot[None, :], 0), axis=1
        )

        attend_base = along_z(attend_weight.reshape(rows_w, 3 * width))
        second_piece = jnp.concatenate([merge_weight.T, expand_weight], axis=1)
        attend_base, second_piece = fence(attend_base, second_piece)
        second_base = along_z(second_piece)
        attend_parts, attend_last = across(attend_base)
        second_base, reduce_piece, attend_last = fence(second_base, reduce_weight.T, attend_last)
        second_parts, second_last = across(second_base)
        reduce_base = along_z(reduce_piece)
        reduce_base, cotangent, second_last = fence(reduce_base, cotangent, second_last)
        reduce_parts, _ = across(reduce_base)

        def spread(array):
            if not staged:
                whole = lax.all_to_all(array, "tensor", split_axis=1, concat_axis=0, tiled=True)
                return whole.reshape(NB, blk, tok)
            own = lax.dynamic_slice(array, (0, t * tok), (width, tok))
            recv = over_x(lax.dynamic_slice(array, (0, (1 - t) * tok), (width, tok)))
            return jnp.concatenate([own, recv], axis=0).reshape(NB, blk, tok)

        def collect(own, other):
            if not staged:
                return lax.all_to_all(
                    own.reshape(D, tok), "tensor", split_axis=0, concat_axis=1, tiled=True
                )
            recv = over_x(other).astype(F32).reshape(width, tok)
            own = own.reshape(width, tok)
            first = jnp.where(t == 0, own, recv)
            last = jnp.where(t == 0, recv, own)
            return jnp.concatenate([first, last], axis=1)

        cond = condition.astype(F32)
        lifted = jax.nn.silu(cond).astype(BF16)
        lifted_cols = lax.all_to_all(lifted, "fsdp", split_axis=1, concat_axis=0, tiled=True)
        mod_weight = modulation_weight.reshape(rows_w, 6 * width)
        mod_part = times(lifted_cols, mod_weight, 1, 0).reshape(FS, group, 6 * width)
        mod_group = jnp.sum(
            lax.all_to_all(mod_part, "fsdp", split_axis=0, concat_axis=0, tiled=True), axis=0
        )
        mod_group = mod_group.reshape(group, 6, width) + modulation_bias.astype(F32)
        if staged:
            own = lax.dynamic_slice(mod_group, (t * images, 0, 0), (images, 6, width))
            recv = over_x(
                lax.dynamic_slice(mod_group, ((1 - t) * images, 0, 0), (images, 6, width))
            )
            mod = jnp.concatenate([own, recv], axis=2)
        else:
            mod = lax.all_to_all(mod_group, "tensor", split_axis=0, concat_axis=2, tiled=True)
        mod = jnp.take(mod.reshape(images, 6, NB, blk), pick, axis=2).reshape(images, 6, D)
        mod = jnp.pad(jnp.swapaxes(mod, 1, 2), ((0, 0), (0, 0), (0, 2)))

        bias_local = jnp.concatenate(
            [attend_bias.reshape(-1), expand_bias, merge_bias, reduce_bias]
        )
        if staged:
            bias_all = jnp.stack([bias_local, over_x(bias_local)], axis=0)
        else:
            bias_all = lax.all_gather(bias_local, "tensor", axis=0, tiled=False)
        bias_all = bias_all.astype(F32)
        at = 2 * width
        zeros = jnp.zeros((T, width), F32)
        attend_b = jnp.concatenate([bias_all[:, :width], zeros, bias_all[:, width:at]], axis=1)
        expand_b = bias_all[:, at : at + hidden]
        at = at + hidden

        def channels(block):
            return jnp.take(block.reshape(NB, blk), pick, axis=0).reshape(D, 1)

        merge_b = channels(bias_all[:, at : at + width])
        reduce_b = channels(bias_all[:, at + width : at + 2 * width])

        grids = lax.dynamic_slice(grid_shapes, (t * images, 0), (images, 2))
        present = grids[:, 0] * grids[:, 1]
        line = jnp.arange(SLOTS, dtype=jnp.int32)
        spots = jnp.stack([line[None, :] // grids[:, 1:2], line[None, :] % grids[:, 1:2]], axis=1)
        spots = jnp.pad(spots, ((0, 0), (0, 6), (0, 0)))
        channel = (order[:, None] * blk + jnp.arange(blk, dtype=jnp.int32)[None, :]).reshape(D)
        quarter = channel // (D // 4)
        within = channel % (D // 4)
        frequency = jnp.exp(within.astype(F32) * (-math.log(10000.0) / (D // 4)))
        angle = jnp.arange(SPOTS, dtype=jnp.int32).astype(F32)[None, :] * frequency[:, None]
        wave = jnp.where((quarter % 2 == 0)[:, None], jnp.sin(angle), jnp.cos(angle))
        high = lax.reduce_precision(wave, 8, 7)
        middle_bits = lax.reduce_precision(wave - high, 8, 7)
        low_bits = lax.reduce_precision(wave - high - middle_bits, 8, 7)
        bits = jnp.concatenate([high, middle_bits, low_bits], axis=1)
        by_row = (quarter < 2)[:, None]
        table = jnp.concatenate(
            [jnp.where(by_row, bits, 0.0), jnp.where(by_row, 0.0, bits)], axis=1
        )
        table = table.astype(BF16).reshape(NB, blk, 6 * SPOTS)

        cube = (NB, blk, tok)
        big = image_rows(NB, blk)
        kept_spec = image_rows(KB, blk)
        stat_spec = pl.BlockSpec((8, SLOTS), lambda i: (0, i))
        act_bytes = D * tok * 4

        tokens_all = spread(tokens)
        cot_all = spread(cotangent)
        residual, features_a, stats_a = pl.pallas_call(
            pre_kernel,
            name="pre",
            grid=(images,),
            in_specs=[
                smem(),
                big,
                pl.BlockSpec((NB, blk, 6 * SPOTS), lambda i: (0, 0, 0)),
                pl.BlockSpec((1, 8, SLOTS), lambda i: (i, 0, 0)),
                column_spec(8),
            ],
            out_specs=[big, big, stat_spec],
            out_shape=[
                jax.ShapeDtypeStruct(cube, F32),
                jax.ShapeDtypeStruct(cube, BF16),
                jax.ShapeDtypeStruct((8, tok), F32),
            ],
            compiler_params=ARB,
            cost_estimate=cost(2 * D * tok * 384, 2 * act_bytes),
        )(pick, tokens_all, table, spots, mod)
        features_a = features_a.reshape(D, tok)

        attend_w = [joined(p, 0, 3 * width) for p in attend_parts]
        head_cube = (heads, HD, tok)
        qkv_spec = pl.BlockSpec((3, heads, HD, SLOTS), lambda i: (0, 0, 0, i))
        head_spec = pl.BlockSpec((heads, HD, SLOTS), lambda i: (0, 0, i))
        log_spec = pl.BlockSpec((heads, SLOTS), lambda i: (0, i))
        qkv, mixture, logs = [], [], []
        for i in range(T):
            projected = times(attend_w[i], features_a, 0, 0) + attend_b[i][:, None]
            qkv.append(projected.astype(BF16).reshape(3, heads, HD, tok))
            mix, log = pl.pallas_call(
                attend_kernel,
                name="attend",
                grid=(images,),
                in_specs=[smem(), qkv_spec],
                out_specs=[head_spec, log_spec],
                out_shape=[
                    jax.ShapeDtypeStruct(head_cube, BF16),
                    jax.ShapeDtypeStruct((heads, tok), F32),
                ],
                compiler_params=ARB,
                cost_estimate=cost(
                    8 * heads * tok * SLOTS * SLOTS, 8 * width * tok, heads * tok * SLOTS
                ),
            )(present, qkv[i])
            mixture.append(mix.reshape(width, tok))
            logs.append(log)
        merge_w = [joined(p, 0, width) for p in second_parts]
        attended = merge_b + sum(times(merge_w[i], mixture[i], 1, 0) for i in range(T))
        attended = attended.reshape(cube)
        middle, features_b, stats_b = pl.pallas_call(
            mid_kernel,
            name="mid",
            grid=(images,),
            in_specs=[big, big, column_spec(8)],
            out_specs=[big, big, stat_spec],
            out_shape=[
                jax.ShapeDtypeStruct(cube, F32),
                jax.ShapeDtypeStruct(cube, BF16),
                jax.ShapeDtypeStruct((8, tok), F32),
            ],
            compiler_params=ARB,
            cost_estimate=cost(10 * D * tok, 4 * act_bytes),
        )(residual, attended, mod)
        features_b = features_b.reshape(D, tok)

        expand_w = [joined(p, width, width + hidden) for p in second_parts]
        expanded = [times(expand_w[i], features_b, 0, 0) + expand_b[i][:, None] for i in range(T)]
        activated = [gelu_tanh(v).astype(BF16) for v in expanded]
        reduce_w = [joined(p, 0, hidden) for p in reduce_parts]
        reduced = reduce_b + sum(times(reduce_w[i], activated[i], 1, 0) for i in range(T))
        kept_cube = (KB, blk, tok)
        other_specs = [kept_spec] if staged else []
        own_out, *other_out, red_grad, cols_out = pl.pallas_call(
            out_kernel if staged else functools.partial(without_other, out_kernel, 6),
            name="out",
            grid=(images,),
            in_specs=[smem(), big, big, big, column_spec(8)],
            out_specs=[kept_spec, *other_specs, big, column_spec(2)],
            out_shape=[
                jax.ShapeDtypeStruct(kept_cube, F32),
                *[jax.ShapeDtypeStruct(kept_cube, BF16) for _ in other_specs],
                jax.ShapeDtypeStruct(cube, BF16),
                jax.ShapeDtypeStruct((images, D, 2), F32),
            ],
            scratch_shapes=[pltpu.VMEM((NB, blk, SLOTS), F32)],
            compiler_params=ARB,
            cost_estimate=cost(10 * D * tok, 4 * act_bytes),
        )(pick, middle, reduced.reshape(cube), cot_all, mod)
        output = collect(own_out, other_out[0] if staged else None)
        red_grad = red_grad.reshape(D, tok)

        def hidden_grad(i, upstream):
            grad = times(reduce_w[i], upstream, 0, 0)
            return jax.vjp(gelu_tanh, expanded[i])[1](grad)[0].astype(BF16)

        reduce_s = Scatter(red_grad, activated).low()
        upstream, reduce_s.state = fence(red_grad, reduce_s.state)
        expand_grad = [hidden_grad(0, upstream)]
        reduce_s.core()
        upstream, expand_grad, reduce_s.state = fence(upstream, expand_grad, reduce_s.state)
        expand_grad = expand_grad + [hidden_grad(i, upstream) for i in range(1, T)]
        reduce_s.first()
        expand_s = Scatter(features_b, expand_grad).low()
        expand_back, expand_s.state, reduce_s.state = fence(
            expand_grad, expand_s.state, reduce_s.state
        )
        features_b_grad = sum(times(expand_w[i], expand_back[i], 1, 0) for i in range(T))
        expand_s.core()
        reduce_s.second()
        features_b_grad, expand_s.state, reduce_s.state = fence(
            features_b_grad, expand_s.state, reduce_s.state
        )
        mid_grad, att_grad, cols_mid = pl.pallas_call(
            back_mid_kernel,
            name="back_mid",
            grid=(images,),
            in_specs=[smem(), big, big, stat_spec, column_spec(8), big, big],
            out_specs=[big, big, column_spec(4)],
            out_shape=[
                jax.ShapeDtypeStruct(cube, F32),
                jax.ShapeDtypeStruct(cube, BF16),
                jax.ShapeDtypeStruct((images, D, 4), F32),
            ],
            compiler_params=ARB,
            cost_estimate=cost(20 * D * tok, 5 * act_bytes),
        )(pick, features_b_grad.reshape(cube), middle, stats_b, mod, cot_all, attended)
        att_grad = att_grad.reshape(D, tok)

        reduce_s.ring()
        expand_s.first()
        att_grad, expand_s.state, reduce_s.state = fence(att_grad, expand_s.state, reduce_s.state)

        merge_s = Scatter(att_grad, mixture).low()
        mix_grad = [
            times(merge_w[i], att_grad, 0, 0).astype(BF16).reshape(head_cube) for i in range(T)
        ]
        reduce_s.ring()
        mix_grad, merge_s.state, reduce_s.state = fence(mix_grad, merge_s.state, reduce_s.state)
        qkv_grad = []
        for i in range(T):
            grads = pl.pallas_call(
                attend_back_kernel,
                name="attend_back",
                grid=(images,),
                in_specs=[smem(), qkv_spec, head_spec, log_spec],
                out_specs=qkv_spec,
                out_shape=jax.ShapeDtypeStruct((3, heads, HD, tok), BF16),
                compiler_params=ARB,
                cost_estimate=cost(
                    20 * heads * tok * SLOTS * SLOTS, 16 * width * tok, heads * tok * SLOTS
                ),
            )(present, qkv[i], mix_grad[i], logs[i])
            qkv_grad.append(grads.reshape(3 * width, tok))
            if i == 0:
                reduce_s.ring()
                merge_s.core()
                qkv_grad, mix_grad, reduce_s.state, merge_s.state = fence(
                    qkv_grad, mix_grad, reduce_s.state, merge_s.state
                )
        expand_s.second()
        merge_s.first()
        attend_s = Scatter(features_a, qkv_grad).low()
        qkv_back, attend_s.state, expand_s.state, merge_s.state = fence(
            qkv_grad, attend_s.state, expand_s.state, merge_s.state
        )
        part = times(attend_w[0], qkv_back[0], 1, 0)
        attend_s.core()
        expand_s.ring()
        part, qkv_back, attend_s.state, expand_s.state = fence(
            part, qkv_back, attend_s.state, expand_s.state
        )
        features_a_grad = part + sum(times(attend_w[i], qkv_back[i], 1, 0) for i in range(1, T))
        attend_s.first()
        merge_s.second()
        expand_s.ring()
        features_a_grad, attend_s.state, merge_s.state, expand_s.state = fence(
            features_a_grad, attend_s.state, merge_s.state, expand_s.state
        )
        own_in, *other_in, cols_pre = pl.pallas_call(
            back_pre_kernel if staged else functools.partial(without_other, back_pre_kernel, 7),
            name="back_pre",
            grid=(images,),
            in_specs=[smem(), big, big, stat_spec, column_spec(8), big],
            out_specs=[kept_spec, *other_specs, column_spec(2)],
            out_shape=[
                jax.ShapeDtypeStruct(kept_cube, F32),
                *[jax.ShapeDtypeStruct(kept_cube, BF16) for _ in other_specs],
                jax.ShapeDtypeStruct((images, D, 2), F32),
            ],
            scratch_shapes=[pltpu.VMEM((NB, blk, SLOTS), F32)],
            compiler_params=ARB,
            cost_estimate=cost(20 * D * tok, 5 * act_bytes),
        )(pick, features_a_grad.reshape(cube), residual, stats_a, mod, mid_grad)
        tokens_grad = collect(own_in, other_in[0] if staged else None)

        expand_s.ring()
        attend_s.second()
        for _ in range(Z - 1):
            merge_s.ring()
            attend_s.ring()
        reduce_wg, expand_wg = reduce_s.done(), expand_s.done()
        merge_wg, attend_wg = merge_s.done(), attend_s.done()

        def own_first(values):
            lead = values.shape[:-1]
            blocks = jnp.take(values.reshape(*lead, NB, blk), back, axis=len(lead))
            return blocks.reshape(*lead, T, width)

        def slot_sums(values):
            return jnp.sum(values.astype(F32), axis=1)

        def total(rows):
            if staged:
                return all_sum(rows[0] + over_x(rows[1]))
            return all_sum(
                lax.psum_scatter(jnp.stack(rows), "tensor", scatter_dimension=0, tiled=True)[0]
            )

        merge_sums = own_first(jnp.sum(cols_mid[:, :, 3], axis=0))
        reduce_sums = own_first(jnp.sum(cols_out[:, :, 1], axis=0))
        hidden_sums = [slot_sums(v) for v in expand_grad]
        early_sum = total(
            [jnp.concatenate([merge_sums[i], hidden_sums[i], reduce_sums[i]]) for i in range(T)]
        )
        qkv_sums = [slot_sums(v) for v in qkv_grad]
        attend_bg = total(
            [jnp.concatenate([v[:width], v[2 * width :]]) for v in qkv_sums]
        )
        merge_bg = early_sum[:width]
        expand_bg = early_sum[width : width + hidden]
        reduce_bg = early_sum[width + hidden :]

        def share(columns):
            grad = own_first(jnp.stack(columns, axis=1).astype(BF16))
            if staged:
                mine, recv = grad[:, :, 0], over_x(grad[:, :, 1])
                grad = jnp.concatenate(
                    [jnp.where(t == 0, mine, recv), jnp.where(t == 0, recv, mine)], axis=0
                )
            else:
                grad = lax.all_to_all(grad, "tensor", split_axis=2, concat_axis=0, tiled=True)
            flat = grad.reshape(1, group, len(columns) * width)
            everyone = lax.all_to_all(
                jnp.broadcast_to(flat, (FS, *flat.shape[1:])),
                "fsdp",
                split_axis=0,
                concat_axis=0,
                tiled=True,
            )
            return everyone.reshape(FS * group, len(columns) * width)

        early = share(
            [cols_mid[:, :, 2], cols_mid[:, :, 0], cols_mid[:, :, 1], cols_out[:, :, 0]]
        )
        late = share([cols_pre[:, :, 0], cols_pre[:, :, 1]])
        cut = 2 * width
        mod_wg = jnp.concatenate(
            [
                times(lifted_cols, late, 0, 0).reshape(rows_w, 2, width),
                times(lifted_cols, early, 0, 0).reshape(rows_w, 4, width),
            ],
            axis=1,
        )
        mod_bg = jnp.concatenate(
            [
                jnp.sum(late.astype(F32), axis=0).reshape(2, width),
                jnp.sum(early.astype(F32), axis=0).reshape(4, width),
            ],
            axis=0,
        )
        lift_part = times(late, mod_weight[:, :cut], 1, 1) + times(early, mod_weight[:, cut:], 1, 1)
        lift_rows = lax.all_to_all(lift_part, "fsdp", split_axis=0, concat_axis=1, tiled=True)
        if staged:
            lift_mine = lax.dynamic_slice(lift_rows, (0, t * width), (group, width))
            lift_sent = lax.dynamic_slice(lift_rows, (0, (1 - t) * width), (group, width))
            lift_grad = lift_mine + over_x(lift_sent)
        else:
            lift_grad = lax.psum_scatter(lift_rows, "tensor", scatter_dimension=1, tiled=True)
        cond_here = lax.dynamic_slice(cond, (0, t * width), (group, width))
        cond_grad = jax.vjp(jax.nn.silu, cond_here)[1](lift_grad)[0]
        return (
            output,
            tokens_grad,
            cond_grad,
            mod_wg,
            mod_bg,
            attend_wg.reshape(rows_w, 3, width),
            attend_bg.reshape(2, width),
            merge_wg.T,
            merge_bg,
            expand_wg,
            expand_bg,
            reduce_wg.T,
            reduce_bg,
        )

    return per_device


def without_other(body, place, *refs):
    return body(*refs[:place], None, *refs[place:])


def solution(mesh):
    return jax.shard_map(
        build(mesh),
        mesh=mesh,
        in_specs=(
            P("tensor", "fsdp"),
            P("fsdp", None),
            P("fsdp", None),
            P("tensor", "fsdp"),
            P("fsdp", None, "tensor"),
            P(None, "tensor"),
            P("fsdp", None, "tensor"),
            P(None, "tensor"),
            P("tensor", "fsdp"),
            P("tensor"),
            P("fsdp", "tensor"),
            P("tensor"),
            P("tensor", "fsdp"),
            P("tensor"),
        ),
        out_specs=(
            P("tensor", "fsdp"),
            P("tensor", "fsdp"),
            P("fsdp", "tensor"),
            P("fsdp", None, "tensor"),
            P(None, "tensor"),
            P("fsdp", None, "tensor"),
            P(None, "tensor"),
            P("tensor", "fsdp"),
            P("tensor"),
            P("fsdp", "tensor"),
            P("tensor"),
            P("tensor", "fsdp"),
            P("tensor"),
        ),
        check_vma=False,
    )
```

```python
import functools
import math

import jax
import jax.numpy as jnp
from jax import lax
from jax.experimental import pallas as pl
from jax.experimental.pallas import tpu as pltpu
from jax.sharding import PartitionSpec as P

D = 1152
HD = 72
SLOTS = 256
EPSILON = 1e-06
NEGATIVE = -1e30
SPOTS = 64
SCALE = 1.0 / math.sqrt(HD)
F32 = jnp.float32
BF16 = jnp.bfloat16


def times(left, right, dim_left, dim_right):
    return lax.dot_general(
        left, right, (((dim_left,), (dim_right,)), ((), ())), preferred_element_type=F32
    )


def fence(*trees):
    return lax.optimization_barrier(trees)


def gelu_tanh(values):
    return jax.nn.gelu(values, approximate=True)


ARB = pltpu.CompilerParams(dimension_semantics=("arbitrary",))


def smem():
    return pl.BlockSpec(memory_space=pltpu.SMEM)


def image_rows(count, width):
    return pl.BlockSpec((count, width, SLOTS), lambda i: (0, 0, i))


def column_spec(width):
    return pl.BlockSpec((1, D, width), lambda i: (i, 0, 0))


def rows_of(ref, i, blk):
    return slice(i * blk, (i + 1) * blk)


def cost(flops, moved, trans=0):
    return pl.CostEstimate(flops=flops, bytes_accessed=moved, transcendentals=trans)


def pre_kernel(idx, tokens, table, spots, mod, res, feat, stats):
    count, blk, _ = tokens.shape
    line = lax.broadcasted_iota(jnp.int32, (6 * SPOTS, SLOTS), 0)
    target = jnp.where(line < 3 * SPOTS, spots[0, 0:1, :], spots[0, 1:2, :])
    onehot = jnp.where((line & (SPOTS - 1)) == target, 1.0, 0.0).astype(BF16)
    total = jnp.zeros((1, SLOTS), F32)
    square = jnp.zeros((1, SLOTS), F32)
    for i in range(count):
        value = tokens[idx[i]].astype(F32) + times(table[i], onehot, 1, 0)
        res[i] = value
        total = total + jnp.sum(value, axis=0, keepdims=True)
        square = square + jnp.sum(value * value, axis=0, keepdims=True)
    center = total * (1.0 / D)
    factor = lax.rsqrt(square * (1.0 / D) - center * center + EPSILON)
    stats[0:1, :] = center
    stats[1:2, :] = factor
    for i in range(count):
        rows = slice(i * blk, (i + 1) * blk)
        normed = (res[i] - center) * factor
        feat[i] = (normed * (1.0 + mod[0, rows, 1:2]) + mod[0, rows, 0:1]).astype(BF16)


def mid_kernel(res, att, mod, mid, feat, stats):
    count, blk, _ = res.shape
    total = jnp.zeros((1, SLOTS), F32)
    square = jnp.zeros((1, SLOTS), F32)
    for i in range(count):
        rows = slice(i * blk, (i + 1) * blk)
        value = res[i] + mod[0, rows, 2:3] * att[i]
        mid[i] = value
        total = total + jnp.sum(value, axis=0, keepdims=True)
        square = square + jnp.sum(value * value, axis=0, keepdims=True)
    center = total * (1.0 / D)
    factor = lax.rsqrt(square * (1.0 / D) - center * center + EPSILON)
    stats[0:1, :] = center
    stats[1:2, :] = factor
    for i in range(count):
        rows = slice(i * blk, (i + 1) * blk)
        normed = (mid[i] - center) * factor
        feat[i] = (normed * (1.0 + mod[0, rows, 4:5]) + mod[0, rows, 3:4]).astype(BF16)


def out_kernel(idx, mid, red, cot, mod, own, other, red_grad, cols, hold):
    count, blk, _ = mid.shape
    for i in range(count):
        rows = slice(i * blk, (i + 1) * blk)
        gate = mod[0, rows, 5:6]
        reduced = red[i]
        upstream = cot[idx[i]].astype(F32)
        hold[idx[i]] = mid[i] + gate * reduced
        rounded = (upstream * gate).astype(BF16)
        red_grad[i] = rounded
        cols[0, rows, 0:1] = jnp.sum(upstream * reduced, axis=1, keepdims=True)
        cols[0, rows, 1:2] = jnp.sum(rounded.astype(F32), axis=1, keepdims=True)
    kept = own.shape[0]
    own[...] = hold[0:kept]
    if other is not None:
        other[...] = hold[kept:count].astype(other.dtype)


def back_mid_kernel(idx, fgrad, mid, stats, mod, cot, att, mid_grad, att_grad, cols):
    count, blk, _ = mid.shape
    center, factor = stats[0:1, :], stats[1:2, :]
    first = jnp.zeros((1, SLOTS), F32)
    second = jnp.zeros((1, SLOTS), F32)
    for i in range(count):
        rows = slice(i * blk, (i + 1) * blk)
        grad = fgrad[i]
        normed = (mid[i] - center) * factor
        both = grad * normed
        scale = 1.0 + mod[0, rows, 4:5]
        cols[0, rows, 0:1] = jnp.sum(grad, axis=1, keepdims=True)
        cols[0, rows, 1:2] = jnp.sum(both, axis=1, keepdims=True)
        first = first + jnp.sum(grad * scale, axis=0, keepdims=True)
        second = second + jnp.sum(both * scale, axis=0, keepdims=True)
    first = first * (1.0 / D)
    second = second * (1.0 / D)
    for i in range(count):
        rows = slice(i * blk, (i + 1) * blk)
        scale = 1.0 + mod[0, rows, 4:5]
        normed = (mid[i] - center) * factor
        value = cot[idx[i]].astype(F32) + factor * (fgrad[i] * scale - first - normed * second)
        mid_grad[i] = value
        rounded = (value * mod[0, rows, 2:3]).astype(BF16)
        att_grad[i] = rounded
        cols[0, rows, 2:3] = jnp.sum(value * att[i], axis=1, keepdims=True)
        cols[0, rows, 3:4] = jnp.sum(rounded.astype(F32), axis=1, keepdims=True)


def back_pre_kernel(idx, fgrad, res, stats, mod, mid_grad, own, other, cols, hold):
    count, blk, _ = res.shape
    center, factor = stats[0:1, :], stats[1:2, :]
    first = jnp.zeros((1, SLOTS), F32)
    second = jnp.zeros((1, SLOTS), F32)
    for i in range(count):
        rows = slice(i * blk, (i + 1) * blk)
        grad = fgrad[i]
        normed = (res[i] - center) * factor
        both = grad * normed
        scale = 1.0 + mod[0, rows, 1:2]
        cols[0, rows, 0:1] = jnp.sum(grad, axis=1, keepdims=True)
        cols[0, rows, 1:2] = jnp.sum(both, axis=1, keepdims=True)
        first = first + jnp.sum(grad * scale, axis=0, keepdims=True)
        second = second + jnp.sum(both * scale, axis=0, keepdims=True)
    first = first * (1.0 / D)
    second = second * (1.0 / D)
    for i in range(count):
        rows = slice(i * blk, (i + 1) * blk)
        scale = 1.0 + mod[0, rows, 1:2]
        normed = (res[i] - center) * factor
        hold[idx[i]] = mid_grad[i] + factor * (fgrad[i] * scale - first - normed * second)
    kept = own.shape[0]
    own[...] = hold[0:kept]
    if other is not None:
        other[...] = hold[kept:count].astype(other.dtype)


def masked_scores(keys, queries, present):
    raw = times(keys, queries, 0, 0) * SCALE
    slot = lax.broadcasted_iota(jnp.int32, raw.shape, 0)
    return jnp.where(slot < present, raw, NEGATIVE)


def attend_kernel(present, qkv, mix, logs):
    here = present[pl.program_id(0)]
    for h in range(mix.shape[0]):
        scores = masked_scores(qkv[1, h], qkv[0, h], here)
        highest = jnp.max(scores, axis=0, keepdims=True)
        weight = jnp.exp(scores - highest)
        total = jnp.sum(weight, axis=0, keepdims=True)
        logs[h : h + 1, :] = highest + jnp.log(total)
        attention = (weight * (1.0 / total)).astype(BF16)
        mix[h] = times(qkv[2, h], attention, 1, 0).astype(BF16)


def attend_back_kernel(present, qkv, mix_grad, logs, grads):
    here = present[pl.program_id(0)]
    for h in range(mix_grad.shape[0]):
        queries, keys, values, upstream = qkv[0, h], qkv[1, h], qkv[2, h], mix_grad[h]
        attention = jnp.exp(masked_scores(keys, queries, here) - logs[h : h + 1, :])
        att_grad = times(values, upstream, 0, 0)
        inner = jnp.sum(attention * att_grad, axis=0, keepdims=True)
        score_grad = (attention * (att_grad - inner)).astype(BF16)
        grads[0, h] = (times(keys, score_grad, 1, 0) * SCALE).astype(BF16)
        grads[1, h] = (times(queries, score_grad, 1, 1) * SCALE).astype(BF16)
        grads[2, h] = times(upstream, attention.astype(BF16), 1, 1).astype(BF16)


def build(mesh):
    FS, T = mesh.shape["fsdp"], mesh.shape["tensor"]
    staged = T == 2 and FS == 16
    Z = FS // 4
    swap_x = [(0, 1), (1, 0)]
    swap_y = [(i, i ^ 2) for i in range(FS)]
    swap_c = [(i, i ^ 1) for i in range(FS)]

    def over_x(v):
        return lax.ppermute(v, "tensor", swap_x)

    def over_y(v):
        return lax.ppermute(v, "fsdp", swap_y)

    def over_c(v):
        return lax.ppermute(v, "fsdp", swap_c)

    def over_z(v, step):
        return lax.ppermute(v, "fsdp", [(i, (i + 4 * step) % FS) for i in range(FS)])

    def along_z(piece):
        if not staged:
            return piece
        return jnp.concatenate([piece] + [over_z(piece, k) for k in range(1, Z)], axis=0)

    class Gather:
        def __init__(self, base):
            self.base, self.near, self.far = base, (), ()

        def first(self):
            if staged:
                self.near = (over_x(self.base), over_y(self.base))

        def second(self):
            if staged:
                half = self.base.shape[0] // 2
                side_x, side_y = self.near
                self.far = (over_x(side_y[:half]), over_y(side_x[half:]))

        def parts(self):
            if not staged:
                whole = lax.all_gather(self.base, "fsdp", axis=0, tiled=True)
                whole = lax.all_gather(whole, "tensor", axis=0, tiled=False)
                return [[whole[i]] for i in range(T)]
            own = [self.base, self.near[1]]
            other = [self.near[0], *self.far]
            return [own + [over_c(v) for v in own], other + [over_c(v) for v in other]]

    def from_all(values):
        return lax.all_to_all(
            jnp.broadcast_to(values[None], (FS, *values.shape)),
            "fsdp",
            split_axis=0,
            concat_axis=0,
            tiled=True,
        )

    class Scatter:
        def __init__(self, left, rights):
            self.left, self.rights, self.recv = left, rights, ()
            start = D // 2 if staged else 0
            self.local = [times(left[start:], r, 1, 1).astype(BF16) for r in rights]
            if staged:
                self.recv = [over_c(v) for v in self.local]

        def core(self, left):
            if not staged:
                return
            own, other = [
                (times(left[: D // 2], r, 1, 1) + v.astype(F32)).astype(BF16)
                for r, v in zip(self.rights, self.recv)
            ]
            quarter, half = D // 8, D // 4
            self.local = [own, other]
            self.recv = (
                over_x(other[half : half + quarter]),
                over_y(other[half + quarter :]),
            )

        def first(self):
            if not staged:
                return
            own, other = self.local
            quarter, half = D // 8, D // 4
            from_x, from_y = self.recv
            send_y = [
                (own[half : half + quarter].astype(F32) + from_x.astype(F32)).astype(BF16),
                own[half + quarter :],
            ]
            send_x = [
                other[:quarter],
                (other[quarter:half].astype(F32) + from_y.astype(F32)).astype(BF16),
            ]
            send_x, send_y = jnp.concatenate(send_x, axis=0), jnp.concatenate(send_y, axis=0)
            self.recv = (over_x(send_x), over_y(send_y))
            self.local = [own[:half], send_x, send_y]

        def second(self):
            if not staged:
                return
            base = self.local[0].astype(F32) + sum(v.astype(F32) for v in self.recv)
            blocks = jnp.split(base, Z, axis=0)
            rounded = [v.astype(BF16) for v in blocks[1:]]
            self.recv = [over_z(rounded[k - 1], Z - k) for k in range(1, Z)]
            self.local = [blocks[0], rounded]

        def third(self):
            if not staged:
                return
            self.local = [self.local[0] + sum(v.astype(F32) for v in self.recv)]

        def done(self):
            if staged:
                return self.local[0]
            part = lax.psum_scatter(
                jnp.stack(self.local), "tensor", scatter_dimension=0, tiled=True
            )[0]
            return lax.psum_scatter(part, "fsdp", scatter_dimension=0, tiled=True).astype(F32)

    def per_device(
        tokens,
        condition,
        grid_shapes,
        cotangent,
        modulation_weight,
        modulation_bias,
        attend_weight,
        attend_bias,
        merge_weight,
        merge_bias,
        expand_weight,
        expand_bias,
        reduce_weight,
        reduce_bias,
    ):
        width = tokens.shape[0]
        hidden = expand_weight.shape[1]
        heads = width // HD
        group = condition.shape[0]
        images = group // T
        tok = images * SLOTS
        t, f = lax.axis_index("tensor"), lax.axis_index("fsdp")
        NB = FS if staged else 16
        blk = D // NB
        KB = NB // T if staged else NB
        rows_w = D // FS

        slot = jnp.arange(NB, dtype=jnp.int32)
        if staged:
            z, y, c = f // 4, (f // 2) % 2, f % 2
            c_rel, y_rel, k_rel = slot // (2 * Z), (slot // Z) % 2, slot % Z
            order = ((z - k_rel + Z) % Z) * 4 + (y ^ y_rel) * 2 + (c ^ c_rel)
            pick = ((order // KB) ^ t) * KB + order % KB
        else:
            order = slot
            pick = slot
        back = jnp.sum(
            jnp.where(pick[None, :] == slot[:, None], slot[None, :], 0), axis=1
        )

        def spread(array):
            if not staged:
                whole = lax.all_to_all(array, "tensor", split_axis=1, concat_axis=0, tiled=True)
                return whole.reshape(NB, blk, tok)
            own = lax.dynamic_slice(array, (0, t * tok), (width, tok))
            recv = over_x(lax.dynamic_slice(array, (0, (1 - t) * tok), (width, tok)))
            return jnp.concatenate([own, recv], axis=0).reshape(NB, blk, tok)

        def collect(own, other):
            if not staged:
                return lax.all_to_all(
                    own.reshape(D, tok), "tensor", split_axis=0, concat_axis=1, tiled=True
                )
            recv = over_x(other).astype(F32).reshape(width, tok)
            own = own.reshape(width, tok)
            first = jnp.where(t == 0, own, recv)
            last = jnp.where(t == 0, recv, own)
            return jnp.concatenate([first, last], axis=1)

        cond = condition.astype(F32)
        lifted = jax.nn.silu(cond).astype(BF16)
        lifted, attend_piece = fence(lifted, attend_weight.reshape(rows_w, 3 * width))
        lifted_cols = lax.all_to_all(lifted, "fsdp", split_axis=1, concat_axis=0, tiled=True)
        mod_weight = modulation_weight.reshape(rows_w, 6 * width)
        room = -3 * width % 128
        attend_g = Gather(
            along_z(
                jnp.concatenate(
                    [jnp.pad(attend_piece, ((0, 0), (0, room))), merge_weight.T], axis=1
                )
            )
        )
        mod_part = times(lifted_cols, mod_weight, 1, 0)
        if staged:
            held = mod_part.reshape(Z, 2, 2, group, 6 * width)
            sent = over_c(jnp.where(c == 0, held[:, :, 1], held[:, :, 0]))
            held = jnp.where(c == 0, held[:, :, 0], held[:, :, 1]) + sent
            sent = over_y(jnp.where(y == 0, held[:, 1], held[:, 0]))
            held = jnp.where(y == 0, held[:, 0], held[:, 1]) + sent
            mod_group = lax.dynamic_index_in_dim(held, z, 0, keepdims=False)
            for k in range(1, Z):
                mod_group = mod_group + over_z(
                    lax.dynamic_index_in_dim(held, (z + k) % Z, 0, keepdims=False), k
                )
        else:
            mod_group = lax.psum_scatter(mod_part, "fsdp", scatter_dimension=0, tiled=True)
        attend_g.first()
        mod_group, expand_piece = fence(mod_group, expand_weight)
        expand_g = Gather(along_z(expand_piece))
        mod_group = mod_group.reshape(group, 6, width) + modulation_bias.astype(F32)
        if staged:
            own = lax.dynamic_slice(mod_group, (t * images, 0, 0), (images, 6, width))
            recv = over_x(
                lax.dynamic_slice(mod_group, ((1 - t) * images, 0, 0), (images, 6, width))
            )
            mod = jnp.concatenate([own, recv], axis=2)
        else:
            mod = lax.all_to_all(mod_group, "tensor", split_axis=0, concat_axis=2, tiled=True)
        mod = jnp.take(mod.reshape(images, 6, NB, blk), pick, axis=2).reshape(images, 6, D)
        mod = jnp.pad(jnp.swapaxes(mod, 1, 2), ((0, 0), (0, 0), (0, 2)))

        bias_local = jnp.concatenate(
            [attend_bias.reshape(-1), expand_bias, merge_bias, reduce_bias]
        )
        if staged:
            bias_all = jnp.stack([bias_local, over_x(bias_local)], axis=0)
        else:
            bias_all = lax.all_gather(bias_local, "tensor", axis=0, tiled=False)
        bias_all = bias_all.astype(F32)
        at = 2 * width
        zeros = jnp.zeros((T, width), F32)
        attend_b = jnp.concatenate([bias_all[:, :width], zeros, bias_all[:, width:at]], axis=1)
        expand_b = bias_all[:, at : at + hidden]
        at = at + hidden

        def channels(block):
            return jnp.take(block.reshape(NB, blk), pick, axis=0).reshape(D, 1)

        merge_b = channels(bias_all[:, at : at + width])
        reduce_b = channels(bias_all[:, at + width : at + 2 * width])

        grids = lax.dynamic_slice(grid_shapes, (t * images, 0), (images, 2))
        present = grids[:, 0] * grids[:, 1]
        line = jnp.arange(SLOTS, dtype=jnp.int32)
        spots = jnp.stack([line[None, :] // grids[:, 1:2], line[None, :] % grids[:, 1:2]], axis=1)
        spots = jnp.pad(spots, ((0, 0), (0, 6), (0, 0)))
        channel = (order[:, None] * blk + jnp.arange(blk, dtype=jnp.int32)[None, :]).reshape(D)
        quarter = channel // (D // 4)
        within = channel % (D // 4)
        frequency = jnp.exp(within.astype(F32) * (-math.log(10000.0) / (D // 4)))
        angle = jnp.arange(SPOTS, dtype=jnp.int32).astype(F32)[None, :] * frequency[:, None]
        wave = jnp.where((quarter % 2 == 0)[:, None], jnp.sin(angle), jnp.cos(angle))
        high = lax.reduce_precision(wave, 8, 7)
        middle_bits = lax.reduce_precision(wave - high, 8, 7)
        low_bits = lax.reduce_precision(wave - high - middle_bits, 8, 7)
        bits = jnp.concatenate([high, middle_bits, low_bits], axis=1)
        by_row = (quarter < 2)[:, None]
        table = jnp.concatenate(
            [jnp.where(by_row, bits, 0.0), jnp.where(by_row, 0.0, bits)], axis=1
        )
        table = table.astype(BF16).reshape(NB, blk, 6 * SPOTS)

        cube = (NB, blk, tok)
        big = image_rows(NB, blk)
        kept_spec = image_rows(KB, blk)
        stat_spec = pl.BlockSpec((8, SLOTS), lambda i: (0, i))
        act_bytes = D * tok * 4

        tokens_all = spread(tokens)
        cot_all = spread(cotangent)
        mod, attend_g.near = fence(mod, attend_g.near)
        attend_g.second()
        residual, features_a, stats_a = pl.pallas_call(
            pre_kernel,
            name="pre",
            grid=(images,),
            in_specs=[
                smem(),
                big,
                pl.BlockSpec((NB, blk, 6 * SPOTS), lambda i: (0, 0, 0)),
                pl.BlockSpec((1, 8, SLOTS), lambda i: (i, 0, 0)),
                column_spec(8),
            ],
            out_specs=[big, big, stat_spec],
            out_shape=[
                jax.ShapeDtypeStruct(cube, F32),
                jax.ShapeDtypeStruct(cube, BF16),
                jax.ShapeDtypeStruct((8, tok), F32),
            ],
            compiler_params=ARB,
            cost_estimate=cost(2 * D * tok * 384, 2 * act_bytes),
        )(pick, tokens_all, table, spots, mod)
        features_a, reduce_piece, expand_g.base = fence(
            features_a.reshape(D, tok), reduce_weight.T, expand_g.base
        )
        reduce_g = Gather(along_z(reduce_piece))
        expand_g.first()

        attend_parts = attend_g.parts()
        attend_all = [jnp.concatenate(p, axis=0) for p in attend_parts]
        attend_w = [v[:, : 3 * width] for v in attend_all]
        merge_w = [v[:, 3 * width + room :] for v in attend_all]
        head_cube = (heads, HD, tok)
        qkv_spec = pl.BlockSpec((3, heads, HD, SLOTS), lambda i: (0, 0, 0, i))
        head_spec = pl.BlockSpec((heads, HD, SLOTS), lambda i: (0, 0, i))
        log_spec = pl.BlockSpec((heads, SLOTS), lambda i: (0, i))
        qkv, mixture, logs = [], [], []
        for i in range(T):
            projected = times(attend_w[i], features_a, 0, 0) + attend_b[i][:, None]
            qkv.append(projected.astype(BF16).reshape(3, heads, HD, tok))
            mix, log = pl.pallas_call(
                attend_kernel,
                name="attend",
                grid=(images,),
                in_specs=[smem(), qkv_spec],
                out_specs=[head_spec, log_spec],
                out_shape=[
                    jax.ShapeDtypeStruct(head_cube, BF16),
                    jax.ShapeDtypeStruct((heads, tok), F32),
                ],
                compiler_params=ARB,
                cost_estimate=cost(
                    8 * heads * tok * SLOTS * SLOTS, 8 * width * tok, heads * tok * SLOTS
                ),
            )(present, qkv[i])
            mixture.append(mix.reshape(width, tok))
            logs.append(log)
            if i == 0:
                features_a, mixture, expand_g.near, reduce_g.base = fence(
                    features_a, mixture, expand_g.near, reduce_g.base
                )
                expand_g.second()
        attended = merge_b + sum(times(merge_w[i], mixture[i], 1, 0) for i in range(T))
        attended, expand_g.far = fence(attended.reshape(cube), expand_g.far)
        reduce_g.first()
        middle, features_b, stats_b = pl.pallas_call(
            mid_kernel,
            name="mid",
            grid=(images,),
            in_specs=[big, big, column_spec(8)],
            out_specs=[big, big, stat_spec],
            out_shape=[
                jax.ShapeDtypeStruct(cube, F32),
                jax.ShapeDtypeStruct(cube, BF16),
                jax.ShapeDtypeStruct((8, tok), F32),
            ],
            compiler_params=ARB,
            cost_estimate=cost(10 * D * tok, 4 * act_bytes),
        )(residual, attended, mod)
        features_b = features_b.reshape(D, tok)

        expand_w = [jnp.concatenate(p, axis=0) for p in expand_g.parts()]
        expanded, activated = [], []
        for i in range(T):
            expanded.append(times(expand_w[i], features_b, 0, 0) + expand_b[i][:, None])
            activated.append(gelu_tanh(expanded[i]).astype(BF16))
            if i == 0:
                features_b, activated, reduce_g.near = fence(
                    features_b, activated, reduce_g.near
                )
                reduce_g.second()
        reduce_w = [jnp.concatenate(p, axis=0) for p in reduce_g.parts()]
        reduced = reduce_b + sum(times(reduce_w[i], activated[i], 1, 0) for i in range(T))
        kept_cube = (KB, blk, tok)
        other_specs = [kept_spec] if staged else []
        own_out, *other_out, red_grad, cols_out = pl.pallas_call(
            out_kernel if staged else functools.partial(without_other, out_kernel, 6),
            name="out",
            grid=(images,),
            in_specs=[smem(), big, big, big, column_spec(8)],
            out_specs=[kept_spec, *other_specs, big, column_spec(2)],
            out_shape=[
                jax.ShapeDtypeStruct(kept_cube, F32),
                *[jax.ShapeDtypeStruct(kept_cube, BF16) for _ in other_specs],
                jax.ShapeDtypeStruct(cube, BF16),
                jax.ShapeDtypeStruct((images, D, 2), F32),
            ],
            scratch_shapes=[pltpu.VMEM((NB, blk, SLOTS), F32)],
            compiler_params=ARB,
            cost_estimate=cost(10 * D * tok, 4 * act_bytes),
        )(pick, middle, reduced.reshape(cube), cot_all, mod)
        red_grad = red_grad.reshape(D, tok)

        def hidden_grad(i, upstream):
            grad = times(reduce_w[i], upstream, 0, 0)
            return jax.vjp(gelu_tanh, expanded[i])[1](grad)[0].astype(BF16)

        reduce_s = Scatter(red_grad, activated)
        upstream, reduce_s.local = fence(red_grad, reduce_s.local)
        expand_grad = [hidden_grad(0, upstream)]
        upstream, expand_grad = fence(upstream, expand_grad)
        reduce_s.core(upstream)
        upstream, reduce_s.local = fence(upstream, reduce_s.local)
        expand_grad = expand_grad + [hidden_grad(i, upstream) for i in range(1, T)]
        expand_grad, reduce_s.local = fence(expand_grad, reduce_s.local)
        reduce_s.first()
        expand_s = Scatter(features_b, expand_grad)
        expand_back, expand_s.local, reduce_s.local = fence(
            expand_grad, expand_s.local, reduce_s.local
        )
        features_b_grad = sum(times(expand_w[i], expand_back[i], 1, 0) for i in range(T))
        features_b_grad, features_b = fence(features_b_grad, features_b)
        expand_s.core(features_b)
        features_b_grad, expand_s.local = fence(features_b_grad, expand_s.local)
        mid_grad, att_grad, cols_mid = pl.pallas_call(
            back_mid_kernel,
            name="back_mid",
            grid=(images,),
            in_specs=[smem(), big, big, stat_spec, column_spec(8), big, big],
            out_specs=[big, big, column_spec(4)],
            out_shape=[
                jax.ShapeDtypeStruct(cube, F32),
                jax.ShapeDtypeStruct(cube, BF16),
                jax.ShapeDtypeStruct((images, D, 4), F32),
            ],
            compiler_params=ARB,
            cost_estimate=cost(20 * D * tok, 5 * act_bytes),
        )(pick, features_b_grad.reshape(cube), middle, stats_b, mod, cot_all, attended)
        att_grad = att_grad.reshape(D, tok)

        att_grad, expand_s.local, reduce_s.local, own_out = fence(
            att_grad, expand_s.local, reduce_s.local, own_out
        )
        output = collect(own_out, other_out[0] if staged else None)
        expand_s.first()
        reduce_s.second()

        merge_s = Scatter(att_grad, mixture)
        mix_grad = [
            times(merge_w[i], att_grad, 0, 0).astype(BF16).reshape(head_cube) for i in range(T)
        ]
        mix_grad, merge_s.local, expand_s.local, reduce_s.local = fence(
            mix_grad, merge_s.local, expand_s.local, reduce_s.local
        )
        qkv_grad = []
        for i in range(T):
            grads = pl.pallas_call(
                attend_back_kernel,
                name="attend_back",
                grid=(images,),
                in_specs=[smem(), qkv_spec, head_spec, log_spec],
                out_specs=qkv_spec,
                out_shape=jax.ShapeDtypeStruct((3, heads, HD, tok), BF16),
                compiler_params=ARB,
                cost_estimate=cost(
                    20 * heads * tok * SLOTS * SLOTS, 16 * width * tok, heads * tok * SLOTS
                ),
            )(present, qkv[i], mix_grad[i], logs[i])
            qkv_grad.append(grads.reshape(3 * width, tok))
            if i == 0:
                qkv_grad, mix_grad, att_grad, reduce_s.local = fence(
                    qkv_grad, mix_grad, att_grad, reduce_s.local
                )
                merge_s.core(att_grad)
                reduce_s.third()
                mix_grad, merge_s.local, reduce_s.local = fence(
                    mix_grad, merge_s.local, reduce_s.local
                )
        qkv_grad, merge_s.local, expand_s.local = fence(qkv_grad, merge_s.local, expand_s.local)
        attend_s = Scatter(features_a, qkv_grad)
        merge_s.first()
        expand_s.second()
        qkv_back, attend_s.local, merge_s.local, expand_s.local = fence(
            qkv_grad, attend_s.local, merge_s.local, expand_s.local
        )
        part = times(attend_w[0], qkv_back[0], 1, 0)
        part, qkv_back, features_a = fence(part, qkv_back, features_a)
        attend_s.core(features_a)
        part, qkv_back, attend_s.local = fence(part, qkv_back, attend_s.local)
        features_a_grad = part + sum(times(attend_w[i], qkv_back[i], 1, 0) for i in range(1, T))
        features_a_grad, attend_s.local, merge_s.local = fence(
            features_a_grad, attend_s.local, merge_s.local
        )
        attend_s.first()
        merge_s.second()
        features_a_grad, attend_s.local, merge_s.local = fence(
            features_a_grad, attend_s.local, merge_s.local
        )
        own_in, *other_in, cols_pre = pl.pallas_call(
            back_pre_kernel if staged else functools.partial(without_other, back_pre_kernel, 7),
            name="back_pre",
            grid=(images,),
            in_specs=[smem(), big, big, stat_spec, column_spec(8), big],
            out_specs=[kept_spec, *other_specs, column_spec(2)],
            out_shape=[
                jax.ShapeDtypeStruct(kept_cube, F32),
                *[jax.ShapeDtypeStruct(kept_cube, BF16) for _ in other_specs],
                jax.ShapeDtypeStruct((images, D, 2), F32),
            ],
            scratch_shapes=[pltpu.VMEM((NB, blk, SLOTS), F32)],
            compiler_params=ARB,
            cost_estimate=cost(20 * D * tok, 5 * act_bytes),
        )(pick, features_a_grad.reshape(cube), residual, stats_a, mod, mid_grad)
        cols_pre, attend_s.local = fence(cols_pre, attend_s.local)
        attend_s.second()
        merge_s.third()
        expand_s.third()
        attend_s.third()
        reduce_wg, expand_wg = reduce_s.done(), expand_s.done()
        merge_wg, attend_wg = merge_s.done(), attend_s.done()

        def own_first(values):
            lead = values.shape[:-1]
            blocks = jnp.take(values.reshape(*lead, NB, blk), back, axis=len(lead))
            return blocks.reshape(*lead, T, width)

        def slot_sums(values):
            return jnp.sum(values.astype(F32), axis=1)

        merge_sums = own_first(jnp.sum(cols_mid[:, :, 3], axis=0))
        reduce_sums = own_first(jnp.sum(cols_out[:, :, 1], axis=0))
        hidden_sums = [slot_sums(v) for v in expand_grad]
        qkv_sums = [slot_sums(v) for v in qkv_grad]
        bias_rows = [
            jnp.concatenate(
                [
                    qkv_sums[i][:width],
                    qkv_sums[i][2 * width :],
                    merge_sums[i],
                    hidden_sums[i],
                    reduce_sums[i],
                ]
            )
            for i in range(T)
        ]
        if staged:
            bias_sum = jnp.sum(from_all(bias_rows[0] + over_x(bias_rows[1])), axis=0)
        else:
            bias_sum = lax.psum_scatter(
                jnp.stack(bias_rows), "tensor", scatter_dimension=0, tiled=True
            )[0]
            bias_sum = lax.psum(bias_sum, "fsdp")
        bounds = [0, 2 * width, 3 * width, 3 * width + hidden, 4 * width + hidden]
        attend_bg, merge_bg, expand_bg, reduce_bg = [
            bias_sum[a:b] for a, b in zip(bounds[:-1], bounds[1:])
        ]

        mod_grad = jnp.stack(
            [
                cols_pre[:, :, 0],
                cols_pre[:, :, 1],
                cols_mid[:, :, 2],
                cols_mid[:, :, 0],
                cols_mid[:, :, 1],
                cols_out[:, :, 0],
            ],
            axis=1,
        ).astype(BF16)
        mod_grad = own_first(mod_grad)
        if staged:
            mine, recv = mod_grad[:, :, 0], over_x(mod_grad[:, :, 1])
            mod_grad = jnp.concatenate(
                [jnp.where(t == 0, mine, recv), jnp.where(t == 0, recv, mine)], axis=0
            )
        else:
            mod_grad = lax.all_to_all(
                mod_grad, "tensor", split_axis=2, concat_axis=0, tiled=True
            )
        mod_grad, other_in = fence(mod_grad, other_in)
        tokens_grad = collect(own_in, other_in[0] if staged else None)
        flat_all = from_all(mod_grad.reshape(group, 6 * width)).reshape(FS * group, 6 * width)
        mod_wg = times(lifted_cols, flat_all, 0, 0).reshape(rows_w, 6, width)
        mod_bg = jnp.sum(flat_all.astype(F32), axis=0).reshape(6, width)
        lift_part = times(flat_all, mod_weight, 1, 1)
        lift_rows = lax.all_to_all(lift_part, "fsdp", split_axis=0, concat_axis=1, tiled=True)
        if staged:
            lift_mine = lax.dynamic_slice(lift_rows, (0, t * width), (group, width))
            lift_sent = lax.dynamic_slice(lift_rows, (0, (1 - t) * width), (group, width))
            lift_grad = lift_mine + over_x(lift_sent)
        else:
            lift_grad = lax.psum_scatter(lift_rows, "tensor", scatter_dimension=1, tiled=True)
        cond_here = lax.dynamic_slice(cond, (0, t * width), (group, width))
        cond_grad = jax.vjp(jax.nn.silu, cond_here)[1](lift_grad)[0]
        return (
            output,
            tokens_grad,
            cond_grad,
            mod_wg,
            mod_bg,
            attend_wg.reshape(rows_w, 3, width),
            attend_bg.reshape(2, width),
            merge_wg.T,
            merge_bg,
            expand_wg,
            expand_bg,
            reduce_wg.T,
            reduce_bg,
        )

    return per_device


def without_other(body, place, *refs):
    return body(*refs[:place], None, *refs[place:])


def solution(mesh):
    return jax.shard_map(
        build(mesh),
        mesh=mesh,
        in_specs=(
            P("tensor", "fsdp"),
            P("fsdp", None),
            P("fsdp", None),
            P("tensor", "fsdp"),
            P("fsdp", None, "tensor"),
            P(None, "tensor"),
            P("fsdp", None, "tensor"),
            P(None, "tensor"),
            P("tensor", "fsdp"),
            P("tensor"),
            P("fsdp", "tensor"),
            P("tensor"),
            P("tensor", "fsdp"),
            P("tensor"),
        ),
        out_specs=(
            P("tensor", "fsdp"),
            P("tensor", "fsdp"),
            P("fsdp", "tensor"),
            P("fsdp", None, "tensor"),
            P(None, "tensor"),
            P("fsdp", None, "tensor"),
            P(None, "tensor"),
            P("tensor", "fsdp"),
            P("tensor"),
            P("fsdp", "tensor"),
            P("tensor"),
            P("tensor", "fsdp"),
            P("tensor"),
        ),
        check_vma=False,
    )
```
